32 devices in a mesh: groups: 2 (over y), band: 4 (over z), head: 4 (over x, core).
Axes of the slice: x: 2, y: 2, z: 4, core: 2. Of those that a mesh axis runs over, the one named last changes fastest.
Arguments:
- latent: bfloat16 [24, 128, 1280], P(('groups', 'band'), None, 'head'), parts along dimension 0, may hold values from -80 to 80
- first_gain: float32 [1280], P('head'), may hold values from 0.1 to 1.9
- first_shift: float32 [1280], P('head'), may hold values from -3 to 3
- kernel: bfloat16 [1280, 3, 3, 1280], P('head'), may hold values from -0.0546875 to 0.0546875
- kernel_bias: float32 [1280], P('head'), may hold values from -3 to 3
- second_gain: float32 [1280], P('head'), may hold values from 0.1 to 1.9
- second_shift: float32 [1280], P('head'), may hold values from -3 to 3
- projection: bfloat16 [1280, 3, 1024], P('band', None, 'head'), may hold values from -0.8385255 to 0.8385255
- output_weight: bfloat16 [1280, 1024], P('head'), may hold values from -0.1875 to 0.1875
- output_bias: float32 [1280], P('head'), may hold values from -3 to 3
Outputs:
- convolved: bfloat16 [24, 128, 1280], P(('groups', 'band'), None, 'head'), parts along dimension 0
- attended: bfloat16 [24, 128, 1280], P(('groups', 'band'), None, 'head'), parts along dimension 0
The draws below stay inside these ranges and needn't reach their ends.
There are 2 independent parts, one for each index of `groups`. The reference program is written for one: setup_inputs(seed, part) draws one part's arguments, and reference() takes and returns one part's arrays. A program takes and returns all parts, laid end to end along the dimension named above; an argument that names none is the same for every part. Nothing has to cross between parts.
All inputs are finite; a program needn't handle non-finite values.
Results may differ from the reference program's by a relative error of at most 0.012.
Values may be sent and summed in bfloat16 or wider, within the bound.
A program may use at most 128 MiB of HBM per device.

```python
import math
import jax
import jax.numpy as jnp
from jax import lax

CHANNELS = 1280
HEADS = 16
HEAD_SIZE = 64
NORM_GROUPS = 32
WIDTH = 128
HEIGHT = 12
INNER = 1024


def draw_latent(key, part):
    first, second = jax.random.split(key, 2)
    place = jnp.arange(HEIGHT).astype(jnp.float32) / max(HEIGHT - 1, 1)
    channel_scale = jnp.exp(jax.random.uniform(second, (CHANNELS,), minval=math.log(0.25), maxval=math.log(2.5)))
    row_scale = jnp.exp(place * math.log(3.0))
    base = jnp.clip(jax.random.normal(first, (HEIGHT, WIDTH, CHANNELS)), -4.0, 4.0)
    return (base * row_scale[:, None, None] * channel_scale).astype(jnp.bfloat16)


def draw_projection(key, part):
    first = jax.random.fold_in(key, 0)
    base = jnp.clip(jax.random.normal(first, (CHANNELS, 3, INNER)), -5.0, 5.0)
    factor = jnp.array([1.3, 1.3, 1.0], jnp.float32)[:, None] * jnp.ones((1, INNER), jnp.float32)
    return (base * factor[None] / math.sqrt(CHANNELS)).astype(jnp.bfloat16)


def block_scale(stream_key, dims, cuts, least, largest):
    level = 1.0
    for dim, shards_of in cuts:
        draws = jax.random.uniform(jax.random.fold_in(jax.random.fold_in(stream_key, 6), dim), (shards_of,), jnp.float32, least / len(cuts), largest / len(cuts))
        level = level * jnp.repeat(jnp.exp(draws), dims[dim] // shards_of).reshape((-1,) + (1,) * (len(dims) - 1 - dim))
    return level


def normal_values(rng, dims, deviation, limit, shards=(), dtype=jnp.bfloat16):
    drawn = jax.random.normal(rng, dims, jnp.float32) * deviation
    if len(shards) > 0:
        drawn = block_scale(rng, dims, shards, -0.22, 0.18) * drawn
    return jnp.clip(drawn, min=-limit, max=limit).astype(dtype)


def setup_inputs(seed: int = 0, part: int = 0) -> dict:
    key_of = jax.random.split(jax.random.key(seed), 11)
    own_keys = jax.random.split(jax.random.fold_in(key_of[10], part), 11)
    return {
        "latent": draw_latent(jax.random.fold_in(jax.random.fold_in(key_of[10], part), 71), part),
        "first_gain": jnp.clip(1.0 + 0.18 * jax.random.normal(key_of[1], (CHANNELS,), jnp.float32), 0.1, 1.9),
        "first_shift": normal_values(key_of[2], (CHANNELS,), 0.5, 3.0, ((0, 4),), jnp.float32),
        "kernel": normal_values(key_of[3], (CHANNELS, 3, 3, CHANNELS), (9 * CHANNELS) ** -0.5, 0.0546875, ((0, 4),)),
        "kernel_bias": normal_values(key_of[4], (CHANNELS,), 0.5, 3.0, ((0, 4),), jnp.float32),
        "second_gain": jnp.clip(1.0 + 0.18 * jax.random.normal(key_of[5], (CHANNELS,), jnp.float32), 0.1, 1.9),
        "second_shift": normal_values(key_of[6], (CHANNELS,), 0.5, 3.0, ((0, 4),), jnp.float32),
        "projection": draw_projection(jax.random.fold_in(key_of[10], 71), part),
        "output_weight": normal_values(key_of[8], (CHANNELS, INNER), INNER ** -0.5, 0.1875, ((0, 4),)),
        "output_bias": normal_values(key_of[9], (CHANNELS,), 0.5, 3.0, ((0, 4),), jnp.float32),
    }


def group_norm(values, gain, shift):
    height, width, channels = values.shape
    grouped = values.reshape(height * width, NORM_GROUPS, channels // NORM_GROUPS)
    mean = lax.optimization_barrier(jnp.mean(grouped, axis=(0, 2)))
    centered = grouped - mean[None, :, None]
    spread = lax.optimization_barrier(jnp.mean(centered * centered, axis=(0, 2)))
    scaled = centered / jnp.sqrt(spread + 1e-05)[None, :, None]
    return scaled.reshape(height, width, channels) * gain + shift

def one_head(operands):
    query, keys, values = operands
    scores = jnp.dot(query, keys.T, preferred_element_type=jnp.float32) * HEAD_SIZE ** (-0.5)
    top = lax.optimization_barrier(jnp.max(scores, axis=1, keepdims=True))
    weights = jnp.exp(scores - top)
    total = lax.optimization_barrier(jnp.sum(weights, axis=1, keepdims=True))
    mixed = jnp.dot(weights.astype(jnp.bfloat16), values, preferred_element_type=jnp.float32)
    return mixed / total

def reference(latent, first_gain, first_shift, kernel, kernel_bias, second_gain, second_shift, projection, output_weight, output_bias):
    latent_wide = latent.astype(jnp.float32)
    activated = jax.nn.silu(group_norm(latent_wide, first_gain, first_shift)).astype(jnp.bfloat16)
    padded = jnp.pad(activated, ((1, 1), (1, 1), (0, 0)))
    summed = jnp.zeros((HEIGHT * WIDTH, CHANNELS), jnp.float32)
    for above in range(3):
        for beside in range(3):
            window = padded[above:above + HEIGHT, beside:beside + WIDTH, :].reshape(HEIGHT * WIDTH, CHANNELS)
            summed = summed + jnp.dot(window, kernel[:, above, beside, :].T, preferred_element_type=jnp.float32)
    convolved = (latent_wide + kernel_bias + summed.reshape(HEIGHT, WIDTH, CHANNELS)).astype(jnp.bfloat16)
    normed = group_norm(convolved.astype(jnp.float32), second_gain, second_shift).astype(jnp.bfloat16)
    tokens = normed.reshape(HEIGHT * WIDTH, CHANNELS)
    projected = jnp.dot(tokens, projection.reshape(CHANNELS, 3 * INNER), preferred_element_type=jnp.float32)
    projected = projected.astype(jnp.bfloat16).reshape(HEIGHT * WIDTH, 3, HEADS, HEAD_SIZE)
    query = jnp.transpose(projected[:, 0], (1, 0, 2))
    keys = jnp.transpose(projected[:, 1], (1, 0, 2))
    values = jnp.transpose(projected[:, 2], (1, 0, 2))
    heads_out = lax.map(one_head, (query, keys, values))
    attention = jnp.transpose(heads_out, (1, 0, 2)).reshape(HEIGHT * WIDTH, INNER).astype(jnp.bfloat16)
    outgoing = jnp.dot(attention, output_weight.T, preferred_element_type=jnp.float32)
    attended = convolved.astype(jnp.float32).reshape(HEIGHT * WIDTH, CHANNELS) + output_bias + outgoing
    return (convolved, attended.reshape(HEIGHT, WIDTH, CHANNELS).astype(jnp.bfloat16))
```

```python
import functools
import math

import jax
import jax.numpy as jnp
from jax import lax
from jax.experimental import pallas as pl
from jax.experimental.pallas import tpu as pltpu
from jax.sharding import PartitionSpec as P

CHANNELS = 1280
HEADS = 16
HEAD_SIZE = 64
NORM_GROUPS = 32


def padded_2(cells, sides, width):
    for axis, dim in sides:
        count = lax.axis_size(axis)
        ends = count - 1
        head = lax.slice_in_dim(cells, 0, width, axis=dim)
        tail = lax.slice_in_dim(cells, cells.shape[dim] - width, cells.shape[dim], axis=dim)
        cells = jnp.concatenate(
            [
                lax.ppermute(tail, axis, [(i, (i + 1) % count) for i in range(ends)]),
                cells,
                lax.ppermute(head, axis, [((i + 1) % count, i) for i in range(ends)]),
            ],
            axis=dim,
        )
    return cells


def normalize(values, gain, shift, group_width, count):
    band_rows, width, channels = values.shape
    grouped = values.reshape(band_rows * width, channels // group_width, group_width)
    mean = lax.psum(jnp.sum(grouped, axis=(0, 2)), "band") / count
    centered = grouped - mean[None, :, None]
    spread = lax.psum(jnp.sum(centered * centered, axis=(0, 2)), "band") / count
    scaled = centered * lax.rsqrt(spread + 1e-05)[None, :, None]
    return scaled.reshape(band_rows, width, channels) * gain + shift


def contract_last(left, right):
    return lax.dot_general(
        left, right, (((1,), (1,)), ((), ())), preferred_element_type=jnp.float32
    )


def kernel_block(padded, weights, band_rows, width):
    inputs = padded.shape[2]
    wide = jnp.pad(padded, ((0, 0), (1, 1), (0, 0)))
    summed = jnp.zeros((band_rows * width, weights.shape[0]), jnp.float32)
    for above in range(3):
        for beside in range(3):
            window = wide[above : above + band_rows, beside : beside + width, :].reshape(
                band_rows * width, inputs
            )
            summed = summed + contract_last(window, weights[:, above, beside, :])
    return summed


def shards(
    latent,
    first_gain,
    first_shift,
    kernel,
    kernel_bias,
    second_gain,
    second_shift,
    projection,
    output_weight,
    output_bias,
):
    band_rows, width, channels = latent.shape
    tokens = band_rows * width
    group_width = CHANNELS // NORM_GROUPS
    count = lax.axis_size("band") * band_rows * width * group_width
    outputs = kernel.shape[0]
    latent_wide = latent.astype(jnp.float32)
    activated = jax.nn.silu(
        normalize(latent_wide, first_gain, first_shift, group_width, count)
    ).astype(jnp.bfloat16)
    gathered = lax.all_gather(activated, "head", axis=2, tiled=True)
    padded = padded_2(gathered, (("band", 0),), 1)
    summed = kernel_block(padded, kernel, band_rows, width)
    convolved = (latent_wide + kernel_bias + summed.reshape(band_rows, width, outputs)).astype(
        jnp.bfloat16
    )
    normed = normalize(
        convolved.astype(jnp.float32), second_gain, second_shift, group_width, count
    ).astype(jnp.bfloat16)
    features = lax.all_gather(normed, "head", axis=2, tiled=True).reshape(tokens, CHANNELS)
    local_inner = projection.shape[2]
    local_heads = local_inner // HEAD_SIZE
    piece = lax.all_gather(projection, "band", axis=0, tiled=True)
    projected = jnp.dot(
        features, piece.reshape(piece.shape[0], 3 * local_inner), preferred_element_type=jnp.float32
    )
    projected = projected.astype(jnp.bfloat16).reshape(tokens, 3, local_inner)
    query = projected[:, 0].reshape(tokens, local_heads, HEAD_SIZE)
    key_value = projected[:, 1:]
    factor = HEAD_SIZE ** (-0.5)
    piece = lax.all_gather(key_value, "band", axis=0, tiled=True)
    running = jnp.full((local_heads, tokens), -1e30, jnp.float32)
    keys = piece[:, 0].reshape(piece.shape[0], local_heads, HEAD_SIZE)
    values = piece[:, 1].reshape(piece.shape[0], local_heads, HEAD_SIZE)
    scores = jnp.einsum("qhd,khd->hqk", query, keys, preferred_element_type=jnp.float32) * factor
    highest = jnp.maximum(running, jnp.max(scores, axis=2))
    weights = jnp.exp(scores - highest[:, :, None])
    total = jnp.sum(weights, axis=2)
    summed_values = jnp.einsum(
        "hqk,khd->hqd", weights.astype(jnp.bfloat16), values, preferred_element_type=jnp.float32
    )
    running, total, summed_values = (highest, total, summed_values)
    attention = (
        jnp.transpose(summed_values / total[:, :, None], (1, 0, 2))
        .reshape(tokens, local_inner)
        .astype(jnp.bfloat16)
    )
    outgoing = contract_last(lax.all_gather(attention, "head", axis=1, tiled=True), output_weight)
    attended = (
        convolved.astype(jnp.float32) + output_bias + outgoing.reshape(band_rows, width, outputs)
    )
    return (convolved, attended.astype(jnp.bfloat16))


def pair_kernel(
    shape,
    lat_hbm,
    gain_a,
    shift_a,
    gain_b,
    shift_b,
    bias_a,
    bias_b,
    kw_hbm,
    pj_hbm,
    ow_hbm,
    wide_ref,
    gain_ref,
    kw,
    pw,
    turned,
    ow,
    par,
    spread_par,
    stat_a,
    stat_b,
    raw_in,
    grid_in,
    sums,
    conv_in,
    feats,
    qkv_out,
    qkv_in,
    att_out,
    att_in,
    vector_0,
    vector_1,
    vector_2,
    vector_3,
    vector_4,
    vector_5,
    local_sem,
    entry_sem,
    send_sem,
    recv_sem,
):
    parts, bands, heads, rows, local, width = shape
    channels = local * heads
    tokens = rows * width
    group_width = CHANNELS // NORM_GROUPS
    groups_here = local // group_width
    pair = 2 * local
    g, b, h = lax.axis_index("groups"), lax.axis_index("band"), lax.axis_index("head")
    sibling = h + 1 - 2 * lax.rem(h, 2)
    cross = lax.rem(h + 2, heads)
    far = lax.rem(sibling + 2, heads)
    has_above, has_below = b > 0, b < bands - 1
    above, below = lax.rem(b + bands - 1, bands), lax.rem(b + 1, bands)
    mesh_id = pl.DeviceIdType.MESH
    used = [0]

    def remote(src, dst, groups=None, band=None, head=None):
        index = used[0]
        used[0] += 1
        return pltpu.make_async_remote_copy(
            src_ref=src,
            dst_ref=dst,
            send_sem=send_sem.at[index],
            recv_sem=recv_sem.at[index],
            device_id=(
                g if groups is None else groups,
                b if band is None else band,
                h if head is None else head,
            ),
            device_id_type=mesh_id,
        )

    opened = []

    def begin(copy, sends=None):
        opened.append((copy, sends))
        if sends is None:
            copy.start()
        else:

            @pl.when(sends)
            def _():
                copy.start()

    def arrive(copy, receives=None):
        if receives is None:
            copy.wait_recv()
        else:

            @pl.when(receives)
            def _():
                copy.wait_recv()

    def channel_rows(shard):
        return pl.ds(pl.multiple_of(shard * local, local), local)

    band_peers = [lax.rem(b + step, bands) for step in range(1, bands)]
    part_peers = [lax.rem(g + step, parts) for step in range(1, parts)]
    mine, crossed, sibs, fars = (channel_rows(s) for s in (h, cross, sibling, far))

    barrier = pltpu.get_barrier_semaphore()
    close = [(g, b, sibling), (g, b, cross), (g, b, far)] + [(peer, b, h) for peer in part_peers]
    for neighbour in close:
        pl.semaphore_signal(barrier, inc=1, device_id=neighbour, device_id_type=mesh_id)

    def tell(sem):
        @pl.when(has_above)
        def _():
            pl.semaphore_signal(sem, inc=1, device_id=(g, above, h), device_id_type=mesh_id)

        @pl.when(has_below)
        def _():
            pl.semaphore_signal(sem, inc=1, device_id=(g, below, h), device_id_type=mesh_id)

    def told(sem, others=0):
        inside = jnp.logical_and(has_above, has_below)

        @pl.when(inside)
        def _():
            pl.semaphore_wait(sem, others + 2)

        @pl.when(jnp.logical_not(inside))
        def _():
            pl.semaphore_wait(sem, others + 1)

    tell(barrier)

    load_lat = pltpu.make_async_copy(lat_hbm, raw_in.at[pl.ds(1, rows), mine, :], local_sem.at[0])
    load_lat.start()
    held_vectors = (vector_0, vector_1, vector_2, vector_3, vector_4, vector_5)
    vectors = (gain_a, shift_a, gain_b, shift_b, bias_a, bias_b)
    load_vectors = [
        pltpu.make_async_copy(vector, held, local_sem.at[4 + index])
        for index, (vector, held) in enumerate(zip(vectors, held_vectors))
    ]
    for load in load_vectors:
        load.start()
    load_kernel = pltpu.make_async_copy(kw_hbm, kw, local_sem.at[1])
    load_rows = pltpu.make_async_copy(pj_hbm, pw.at[:, channel_rows(b), :], local_sem.at[2])
    load_output = pltpu.make_async_copy(ow_hbm, ow, local_sem.at[3])
    load_kernel.start()
    load_rows.start()
    load_output.start()

    count = rows * width * group_width
    both = 2 * groups_here
    sub16 = lax.broadcasted_iota(jnp.int32, (both, width), 0)
    lane16 = lax.broadcasted_iota(jnp.int32, (both, width), 1)
    sub8 = lax.broadcasted_iota(jnp.int32, (groups_here, width), 0)
    lane8 = lax.broadcasted_iota(jnp.int32, (groups_here, width), 1)

    def statistics(buffer, first):
        values = [
            buffer[first + row, mine, :].astype(jnp.float32).reshape(groups_here, group_width, width)
            for row in range(rows)
        ]
        total = sum(jnp.sum(value, axis=1) for value in values)
        mean = jnp.sum(total, axis=1, keepdims=True) / count
        mean = jnp.broadcast_to(mean, (groups_here, width))
        squares = 0.0
        for value in values:
            centered = value - mean[:, None, :]
            squares = squares + jnp.sum(centered * centered, axis=1)
        squares = jnp.broadcast_to(jnp.sum(squares, axis=1, keepdims=True), (groups_here, width))
        stacked = jnp.concatenate([mean, squares], axis=0)
        return jnp.sum(jnp.where(sub16 == lane16, stacked, 0.0), axis=0, keepdims=True)

    def combined(stat):
        found = []
        for shard in (h, sibling, cross, far):
            pieces = [stat[band * heads + shard] for band in range(bands)]
            total = sum(pieces)
            mean = total / bands
            offsets = sum((piece - mean) * (piece - mean) for piece in pieces)
            spread = pltpu.roll(jnp.broadcast_to(total, (8, width)), width - groups_here, 1)[:1]
            scale = lax.rsqrt((spread + offsets * count) / (count * bands) + 1e-05)
            pair_of = []
            for line in (mean, scale):
                wide = jnp.broadcast_to(line, (groups_here, width))
                column = jnp.sum(jnp.where(sub8 == lane8, wide, 0.0), axis=1, keepdims=True)
                pair_of.append(jnp.broadcast_to(column, (groups_here, width)))
            found.append(pair_of)
        return found

    def normalized(value, stats, which, span):
        mean, scale = stats
        grouped = value.astype(jnp.float32).reshape(groups_here, group_width, width)
        scaled = (grouped - mean[:, None, :]) * scale[:, None, :]
        return scaled.reshape(local, width) * spread_par[2 * which, span, :] + spread_par[
            2 * which + 1, span, :
        ]

    load_lat.wait()
    stat_a[b * heads + h] = statistics(raw_in, 1)
    for index, load in enumerate(load_vectors):
        load.wait()
        par[h, index] = held_vectors[index][...].reshape(1, local)

    told(barrier, len(close))

    def gather_pieces(buffer, pieces):
        sent = []
        for piece in pieces:
            own = buffer.at[piece, mine, :]
            there = buffer.at[piece, crossed, :]
            sent.append(
                (
                    remote(own, own, head=cross),
                    remote(own, own, head=sibling),
                    remote(there, there, head=sibling),
                )
            )
        return sent

    own_row = stat_a.at[b * heads + h]
    near_stats = [remote(own_row, own_row, head=peer) for peer in (cross, far, sibling)]
    near_par = [
        remote(par.at[h, pl.ds(0, 4)], par.at[h, pl.ds(0, 4)], head=peer)
        for peer in (cross, far, sibling)
    ]
    edges = (pl.ds(rows, 1), pl.ds(1, 1), pl.ds(2, rows - 2))
    gathered = gather_pieces(raw_in, edges)
    halo = []
    for source, target, peer, sends, receives in (
        (rows, 0, below, has_below, has_above),
        (1, rows + 1, above, has_above, has_below),
    ):
        for shard in (mine, crossed):
            move = remote(raw_in.at[source, shard, :], raw_in.at[target, shard, :], band=peer)
            onward = raw_in.at[target, shard, :]
            halo.append((move, remote(onward, onward, head=sibling), sends, receives))
    for copy in near_stats:
        begin(copy)
    tell(entry_sem.at[0])
    for to_cross, to_sibling, _ in gathered:
        begin(to_cross)
        begin(to_sibling)
    for index in (0, 2):
        move, _, sends, _ = halo[index]
        begin(move, sends)
    for copy in near_par:
        begin(copy)

    share = local // parts

    def share_rows(band, part):
        return pl.ds(pl.multiple_of(band * local + part * share, share), share)

    hops = []
    passed = []
    for kind in range(3):
        steps = []
        for hop in range(1, bands):
            two = []
            for sign, peer in ((1, below), (-1, above)):
                held = lax.rem(b - sign * (hop - 1) + bands, bands)
                got = lax.rem(b - sign * hop + bands, bands)
                if sign > 0:
                    sends = jnp.logical_and(b < bands - 1, b >= hop - 1)
                    receives = b >= hop
                else:
                    sends = jnp.logical_and(b > 0, b + hop - 1 < bands)
                    receives = b + hop < bands
                if hop == 1:
                    source = pj_hbm.at[kind, pl.ds(pl.multiple_of(g * share, share), share), :]
                else:
                    source = pw.at[kind, share_rows(held, g), :]
                move = remote(source, pw.at[kind, share_rows(held, g), :], band=peer)
                two.append((move, sends, receives, got))
            steps.append(two)
        hops.append(steps)
        passed.append([])

    def send_hop(kind, index):
        for move, sends, _, _ in hops[kind][index]:
            begin(move, sends)

    def take_hop(kind, index):
        for move, _, receives, _ in hops[kind][index]:
            arrive(move, receives)
        if index + 1 < len(hops[kind]):
            send_hop(kind, index + 1)
        for _, _, receives, got in hops[kind][index]:
            onward = pw.at[kind, share_rows(got, g), :]
            for peer in part_peers:
                move = remote(onward, onward, groups=peer)
                begin(move, receives)
                passed[kind].append((move, receives))

    order = (1, 2, 0)
    last = len(hops[0])
    steps_due = [(kind, index) for index in range(last) for kind in order]

    def take_next(number):
        for _ in range(number):
            if steps_due:
                take_hop(*steps_due.pop(0))

    for kind in order:
        send_hop(kind, 0)

    for copy in near_stats:
        arrive(copy)
    told(entry_sem.at[0])
    tell(entry_sem.at[1])
    told(entry_sem.at[1])
    block = stat_a.at[pl.ds(b * heads, heads)]
    band_stats = [remote(block, block, band=peer) for peer in band_peers]
    for copy in band_stats:
        begin(copy)

    for copy in near_par:
        arrive(copy)
    blocks = -(-local // width)
    lines = []
    for shard in range(heads):
        for index in range(4):
            lines.append(par[shard, index])
    lines += [par[h, 4], par[h, 5]]
    gap = jnp.zeros((1, blocks * width - local), jnp.float32)
    flat = []
    for line in lines:
        line = jnp.concatenate([line, gap], axis=1)
        flat += [line[:, k * width : (k + 1) * width] for k in range(blocks)]
    flat.append(jnp.zeros((-len(flat) % width, width), jnp.float32))
    columns = jnp.concatenate(flat, axis=0).T

    def column(index):
        pieces = [columns[:, index * blocks + k : index * blocks + k + 1] for k in range(blocks)]
        return jnp.broadcast_to(jnp.concatenate(pieces, axis=0)[:local], (local, width))

    for index in range(4):
        for shard in range(heads):
            spread_par[index, shard * local : (shard + 1) * local, :] = column(shard * 4 + index)
    for index in range(2):
        spread_par[4 + index, :local, :] = column(heads * 4 + index)

    for index in range(2):
        to_cross, _, onward = gathered[index]
        arrive(to_cross)
        begin(onward)
        move, _, sends, _ = halo[2 * index + 1]
        begin(move, sends)
    for index in (0, 2):
        move, onward, _, receives = halo[index]
        arrive(move, receives)
        begin(onward, receives)
    for target, receives in ((0, has_above), (rows + 1, has_below)):

        @pl.when(jnp.logical_not(receives))
        def _(target=target):
            grid_in[target] = jnp.zeros((channels, width), jnp.bfloat16)

    take_next(1)
    to_cross, _, onward = gathered[2]
    arrive(to_cross)
    begin(onward)
    for copy in band_stats:
        arrive(copy)
    first = combined(stat_a)

    def activate(row, slot, span):
        value = 0.5 * normalized(raw_in[row, span, :], first[slot], 0, span)
        grid_in[row, span, :] = (value + value * jnp.tanh(value)).astype(jnp.bfloat16)

    def activate_edge(target, receives, slots):
        @pl.when(receives)
        def _():
            for slot, span in slots:
                activate(target, slot, span)

    def half(which):
        return pl.ds(pl.multiple_of(which * pair, pair), pair)

    def convolve(which, overs, fresh):
        span = half(which)
        total = None
        for over in overs:
            window = jnp.concatenate([grid_in[over + row, span, :] for row in range(rows)], axis=1)
            weights = kw[over, :, :, span].reshape(3 * local, pair)
            part = jnp.dot(weights, window, preferred_element_type=jnp.float32)
            total = part if total is None else total + part
        if not fresh:
            total = sums[...] + total
        sums[...] = total

    this_half, other_half = h // 2, cross // 2
    near_slots = ((0, mine), (1, sibs))
    far_slots = ((2, crossed), (3, fars))
    for _, to_sibling, _ in gathered:
        arrive(to_sibling)
    for row in range(rows):
        for slot, span in near_slots:
            activate(1 + row, slot, span)
    take_next(1)
    load_kernel.wait()
    convolve(this_half, (1,), True)
    for index in (0, 2):
        _, onward, _, receives = halo[index]
        arrive(onward, receives)
    activate_edge(0, has_above, near_slots)
    activate_edge(rows + 1, has_below, near_slots)
    for index in (1, 3):
        move, onward, _, receives = halo[index]
        arrive(move, receives)
        begin(onward, receives)
    convolve(this_half, (0, 2), False)
    take_next(2)
    for _, _, onward in gathered:
        arrive(onward)
    for row in range(rows):
        for slot, span in far_slots:
            activate(1 + row, slot, span)
    convolve(other_half, (1,), False)
    for index in (1, 3):
        _, onward, _, receives = halo[index]
        arrive(onward, receives)
    activate_edge(0, has_above, far_slots)
    activate_edge(rows + 1, has_below, far_slots)
    take_next(1)
    convolve(other_half, (0, 2), False)

    place = lax.broadcasted_iota(jnp.int32, (local, width), 1)
    normed = gather_pieces(conv_in, tuple(pl.ds(row, 1) for row in range(rows)))
    for row in range(rows):
        span = slice(row * width, (row + 1) * width)
        left = jnp.where(place == 0, 0.0, pltpu.roll(sums[:local, span], 1, 1))
        right = jnp.where(place == width - 1, 0.0, pltpu.roll(sums[2 * local :, span], width - 1, 1))
        value = (
            raw_in[1 + row, mine, :].astype(jnp.float32)
            + spread_par[4, :local, :]
            + (sums[local : 2 * local, span] + left + right)
        )
        wide_ref[row] = value
        conv_in[row, mine, :] = value.astype(jnp.bfloat16)
        begin(normed[row][0])
        begin(normed[row][1])

    stat_b[b * heads + h] = statistics(conv_in, 0)
    own_row = stat_b.at[b * heads + h]
    all_stats = [
        remote(own_row, own_row, band=lax.rem(b + up, bands), head=lax.rem(h + over, heads))
        for up in range(bands - 1, -1, -1)
        for over in range(heads - 1, -1, -1)
        if up or over
    ]
    for copy in all_stats:
        begin(copy)
    load_rows.wait()
    take_next(2)
    arrive(normed[0][0])
    begin(normed[0][2])
    for copy in all_stats:
        arrive(copy)
    second = combined(stat_b)
    arrive(normed[1][0])
    begin(normed[1][2])
    for move, receives in passed[1]:
        arrive(move, receives)

    def normalize_row(row):
        arrive(normed[row][1])
        span = slice(row * width, (row + 1) * width)
        for slot, shard in ((0, mine), (1, sibs), (2, crossed)):
            feats[shard, span] = normalized(conv_in[row, shard, :], second[slot], 1, shard).astype(
                jnp.bfloat16
            )
        arrive(normed[row][2])
        feats[fars, span] = normalized(conv_in[row, fars, :], second[3], 1, fars).astype(jnp.bfloat16)

    def project(kind, span):
        return jnp.dot(turned[kind], feats[:, span], preferred_element_type=jnp.float32).astype(
            jnp.bfloat16
        )

    def place_heads(kind, made, chosen):
        for head in range(bands):
            for index, row in enumerate(chosen):
                qkv_out[kind, head, row] = made[
                    head * HEAD_SIZE : (head + 1) * HEAD_SIZE, index * width : (index + 1) * width
                ]

    def spread_rows(kind, row, size):
        chosen = pl.ds(row, size)
        qkv_in[kind, b, chosen] = qkv_out[kind, b, chosen]
        moves = [
            remote(qkv_out.at[kind, peer, chosen], qkv_in.at[kind, b, chosen], band=peer)
            for peer in band_peers
        ]
        for copy in moves:
            begin(copy)
        return moves

    turned[1] = pw[1].T
    moved_keys = []
    for row in range(rows):
        normalize_row(row)
        if row + 2 < rows:
            arrive(normed[row + 2][0])
            begin(normed[row + 2][2])
        place_heads(1, project(1, slice(row * width, (row + 1) * width)), (row,))
        moved_keys += spread_rows(1, row, 1)
        take_next(1)
    take_next(len(steps_due))
    everything = slice(0, tokens)
    for move, receives in passed[2]:
        arrive(move, receives)
    turned[2] = pw[2].T
    place_heads(2, project(2, everything), range(rows))
    moved_values = spread_rows(2, 0, rows)
    for move, receives in passed[0]:
        arrive(move, receives)
    turned[0] = pw[0].T
    place_heads(0, project(0, everything), range(rows))
    moved_queries = [spread_rows(0, row, 1) for row in range(rows)]

    inner = bands * HEAD_SIZE
    factor = HEAD_SIZE ** (-0.5) * math.log2(math.e)

    def feature_rows(shard):
        return pl.ds(pl.multiple_of(shard * inner, inner), inner)

    own_features = pl.ds(pl.multiple_of(h * inner + b * HEAD_SIZE, HEAD_SIZE), HEAD_SIZE)
    returned = [
        [
            remote(att_out.at[row, peer], att_in.at[row, own_features, :], band=peer)
            for peer in band_peers
        ]
        for row in range(rows)
    ]
    final = []
    for row in range(rows):
        own = att_in.at[row, feature_rows(h), :]
        there = att_in.at[row, feature_rows(cross), :]
        final.append(
            (
                remote(own, own, head=cross),
                remote(own, own, head=sibling),
                remote(there, there, head=sibling),
            )
        )

    def pass_on(row):
        for copy in returned[row]:
            arrive(copy)
        begin(final[row][0])
        begin(final[row][1])

    def relay(row):
        arrive(final[row][0])
        begin(final[row][2])

    def finish(row):
        arrive(final[row][1])
        arrive(final[row][2])
        outgoing = jnp.dot(ow[...], att_in[row], preferred_element_type=jnp.float32)
        gain_ref[row] = (
            conv_in[row, mine, :].astype(jnp.float32) + spread_par[5, :local, :] + outgoing
        )

    for copy in moved_keys:
        arrive(copy)
    keys = jnp.concatenate(
        [qkv_in[1, source, row] for source in range(bands) for row in range(rows)], axis=1
    ).T
    for copy in moved_values:
        arrive(copy)
    values = jnp.concatenate(
        [qkv_in[2, source, row] for source in range(bands) for row in range(rows)], axis=1
    )
    for row in range(rows):
        for copy in moved_queries[row]:
            arrive(copy)
        query = jnp.concatenate([qkv_in[0, source, row] for source in range(bands)], axis=1)
        scores = jnp.dot(keys, query, preferred_element_type=jnp.float32)
        top = jnp.max(scores, axis=0, keepdims=True)
        heavy = jnp.exp2((scores - top) * factor)
        total = jnp.sum(heavy, axis=0, keepdims=True)
        mixed = jnp.dot(values, heavy.astype(jnp.bfloat16), preferred_element_type=jnp.float32)
        result = (mixed / total).astype(jnp.bfloat16)
        for source in range(bands):
            att_out[row, source] = result[:, source * width : (source + 1) * width]
        for copy in returned[row]:
            begin(copy)
        att_in[row, own_features, :] = att_out[row, b]
        if row >= 1:
            pass_on(row - 1)
        if row >= 2:
            relay(row - 2)
    load_output.wait()
    pass_on(rows - 1)
    if rows >= 2:
        relay(rows - 2)
    for row in range(rows - 1):
        finish(row)
    relay(rows - 1)
    finish(rows - 1)

    for copy, sends in opened:
        if sends is None:
            copy.wait_send()
        else:

            @pl.when(sends)
            def _(copy=copy):
                copy.wait_send()


def pair_shards(
    parts,
    bands,
    heads,
    latent,
    first_gain,
    first_shift,
    kernel,
    kernel_bias,
    second_gain,
    second_shift,
    projection,
    output_weight,
    output_bias,
):
    rows, width, local = latent.shape
    channels, tokens = local * heads, rows * width
    inner = projection.shape[2]
    vectors = [first_gain, first_shift, second_gain, second_shift, kernel_bias, output_bias]
    vmem = pl.BlockSpec(memory_space=pltpu.VMEM)
    hbm = pl.BlockSpec(memory_space=pl.ANY)
    result = jax.ShapeDtypeStruct((rows, local, width), jnp.float32)
    copies = 160
    call = pl.pallas_call(
        functools.partial(pair_kernel, (parts, bands, heads, rows, local, width)),
        out_shape=(result, result),
        in_specs=[hbm] * 10,
        out_specs=(vmem, vmem),
        scratch_shapes=[
            pltpu.VMEM((3, 3, local, channels), jnp.bfloat16),
            pltpu.VMEM((3, channels, inner), jnp.bfloat16),
            pltpu.VMEM((3, inner, channels), jnp.bfloat16),
            pltpu.VMEM((local, inner * heads), jnp.bfloat16),
            pltpu.VMEM((heads, 6, 1, local), jnp.float32),
            pltpu.VMEM((6, channels, width), jnp.float32),
            pltpu.VMEM((bands * heads, 1, width), jnp.float32),
            pltpu.VMEM((bands * heads, 1, width), jnp.float32),
            pltpu.VMEM((rows + 2, channels, width), jnp.bfloat16),
            pltpu.VMEM((rows + 2, channels, width), jnp.bfloat16),
            pltpu.VMEM((3 * local, tokens), jnp.float32),
            pltpu.VMEM((rows, channels, width), jnp.bfloat16),
            pltpu.VMEM((channels, tokens), jnp.bfloat16),
            pltpu.VMEM((3, bands, rows, HEAD_SIZE, width), jnp.bfloat16),
            pltpu.VMEM((3, bands, rows, HEAD_SIZE, width), jnp.bfloat16),
            pltpu.VMEM((rows, bands, HEAD_SIZE, width), jnp.bfloat16),
            pltpu.VMEM((rows, inner * heads, width), jnp.bfloat16),
        ]
        + [pltpu.VMEM((local,), jnp.float32)] * 6
        + [
            pltpu.SemaphoreType.DMA((10,)),
            pltpu.SemaphoreType.REGULAR((2,)),
            pltpu.SemaphoreType.DMA((copies,)),
            pltpu.SemaphoreType.DMA((copies,)),
        ],
        compiler_params=pltpu.CompilerParams(
            collective_id=0, has_side_effects=True, vmem_limit_bytes=60 << 20
        ),
    )
    wide, gained = call(
        jnp.transpose(latent, (0, 2, 1)),
        *vectors,
        jnp.transpose(kernel, (1, 2, 0, 3)),
        jnp.transpose(projection, (1, 0, 2)),
        output_weight,
    )
    convolved = jnp.transpose(wide, (0, 2, 1)).astype(jnp.bfloat16)
    return convolved, jnp.transpose(gained, (0, 2, 1)).astype(jnp.bfloat16)


def solution(mesh):
    placed = (
        P(("groups", "band"), None, "head"),
        P("head"),
        P("head"),
        P("head", None, None, None),
        P("head"),
        P("head"),
        P("head"),
        P("band", None, "head"),
        P("head", None),
        P("head"),
    )
    parts, bands, heads = (mesh.shape[axis] for axis in ("groups", "band", "head"))
    paired = heads == 4 and bands > 1 and HEADS == heads * bands and CHANNELS % (16 * parts * heads) == 0
    body = functools.partial(pair_shards, parts, bands, heads) if paired else shards
    return jax.shard_map(
        body,
        mesh=mesh,
        in_specs=placed,
        out_specs=(P(("groups", "band"), None, "head"), P(("groups", "band"), None, "head")),
        check_vma=False,
    )
```

```python
import functools
import math

import jax
import jax.numpy as jnp
from jax import lax
from jax.experimental import pallas as pl
from jax.experimental.pallas import tpu as pltpu
from jax.sharding import PartitionSpec as P

CHANNELS = 1280
HEADS = 16
HEAD_SIZE = 64
NORM_GROUPS = 32


def padded_2(cells, sides, width):
    for axis, dim in sides:
        count = lax.axis_size(axis)
        ends = count - 1
        head = lax.slice_in_dim(cells, 0, width, axis=dim)
        tail = lax.slice_in_dim(cells, cells.shape[dim] - width, cells.shape[dim], axis=dim)
        cells = jnp.concatenate(
            [
                lax.ppermute(tail, axis, [(i, (i + 1) % count) for i in range(ends)]),
                cells,
                lax.ppermute(head, axis, [((i + 1) % count, i) for i in range(ends)]),
            ],
            axis=dim,
        )
    return cells


def normalize(values, gain, shift, group_width, count):
    band_rows, width, channels = values.shape
    grouped = values.reshape(band_rows * width, channels // group_width, group_width)
    mean = lax.psum(jnp.sum(grouped, axis=(0, 2)), "band") / count
    centered = grouped - mean[None, :, None]
    spread = lax.psum(jnp.sum(centered * centered, axis=(0, 2)), "band") / count
    scaled = centered * lax.rsqrt(spread + 1e-05)[None, :, None]
    return scaled.reshape(band_rows, width, channels) * gain + shift


def contract_last(left, right):
    return lax.dot_general(
        left, right, (((1,), (1,)), ((), ())), preferred_element_type=jnp.float32
    )


def kernel_block(padded, weights, band_rows, width):
    inputs = padded.shape[2]
    wide = jnp.pad(padded, ((0, 0), (1, 1), (0, 0)))
    summed = jnp.zeros((band_rows * width, weights.shape[0]), jnp.float32)
    for above in range(3):
        for beside in range(3):
            window = wide[above : above + band_rows, beside : beside + width, :].reshape(
                band_rows * width, inputs
            )
            summed = summed + contract_last(window, weights[:, above, beside, :])
    return summed


def shards(
    latent,
    first_gain,
    first_shift,
    kernel,
    kernel_bias,
    second_gain,
    second_shift,
    projection,
    output_weight,
    output_bias,
):
    band_rows, width, channels = latent.shape
    tokens = band_rows * width
    group_width = CHANNELS // NORM_GROUPS
    count = lax.axis_size("band") * band_rows * width * group_width
    outputs = kernel.shape[0]
    latent_wide = latent.astype(jnp.float32)
    activated = jax.nn.silu(
        normalize(latent_wide, first_gain, first_shift, group_width, count)
    ).astype(jnp.bfloat16)
    gathered = lax.all_gather(activated, "head", axis=2, tiled=True)
    padded = padded_2(gathered, (("band", 0),), 1)
    summed = kernel_block(padded, kernel, band_rows, width)
    convolved = (latent_wide + kernel_bias + summed.reshape(band_rows, width, outputs)).astype(
        jnp.bfloat16
    )
    normed = normalize(
        convolved.astype(jnp.float32), second_gain, second_shift, group_width, count
    ).astype(jnp.bfloat16)
    features = lax.all_gather(normed, "head", axis=2, tiled=True).reshape(tokens, CHANNELS)
    local_inner = projection.shape[2]
    local_heads = local_inner // HEAD_SIZE
    piece = lax.all_gather(projection, "band", axis=0, tiled=True)
    projected = jnp.dot(
        features, piece.reshape(piece.shape[0], 3 * local_inner), preferred_element_type=jnp.float32
    )
    projected = projected.astype(jnp.bfloat16).reshape(tokens, 3, local_inner)
    query = projected[:, 0].reshape(tokens, local_heads, HEAD_SIZE)
    key_value = projected[:, 1:]
    factor = HEAD_SIZE ** (-0.5)
    piece = lax.all_gather(key_value, "band", axis=0, tiled=True)
    running = jnp.full((local_heads, tokens), -1e30, jnp.float32)
    keys = piece[:, 0].reshape(piece.shape[0], local_heads, HEAD_SIZE)
    values = piece[:, 1].reshape(piece.shape[0], local_heads, HEAD_SIZE)
    scores = jnp.einsum("qhd,khd->hqk", query, keys, preferred_element_type=jnp.float32) * factor
    highest = jnp.maximum(running, jnp.max(scores, axis=2))
    weights = jnp.exp(scores - highest[:, :, None])
    total = jnp.sum(weights, axis=2)
    summed_values = jnp.einsum(
        "hqk,khd->hqd", weights.astype(jnp.bfloat16), values, preferred_element_type=jnp.float32
    )
    running, total, summed_values = (highest, total, summed_values)
    attention = (
        jnp.transpose(summed_values / total[:, :, None], (1, 0, 2))
        .reshape(tokens, local_inner)
        .astype(jnp.bfloat16)
    )
    outgoing = contract_last(lax.all_gather(attention, "head", axis=1, tiled=True), output_weight)
    attended = (
        convolved.astype(jnp.float32) + output_bias + outgoing.reshape(band_rows, width, outputs)
    )
    return (convolved, attended.astype(jnp.bfloat16))


def pair_kernel(
    shape,
    lat_hbm,
    gain_a,
    shift_a,
    gain_b,
    shift_b,
    bias_a,
    bias_b,
    kw_hbm,
    pj_hbm,
    ow_hbm,
    wide_ref,
    gain_ref,
    kw,
    pw,
    turned,
    ow,
    par,
    spread_par,
    stat_a,
    stat_b,
    raw_in,
    grid_in,
    sums,
    conv_in,
    feats,
    qkv_out,
    qkv_in,
    att_out,
    att_in,
    vector_0,
    vector_1,
    vector_2,
    vector_3,
    vector_4,
    vector_5,
    local_sem,
    entry_sem,
    send_sem,
    recv_sem,
):
    parts, bands, heads, rows, local, width = shape
    channels = local * heads
    tokens = rows * width
    group_width = CHANNELS // NORM_GROUPS
    groups_here = local // group_width
    pair = 2 * local
    g, b, h = lax.axis_index("groups"), lax.axis_index("band"), lax.axis_index("head")
    sibling = h + 1 - 2 * lax.rem(h, 2)
    cross = lax.rem(h + 2, heads)
    far = lax.rem(sibling + 2, heads)
    has_above, has_below = b > 0, b < bands - 1
    above, below = lax.rem(b + bands - 1, bands), lax.rem(b + 1, bands)
    mesh_id = pl.DeviceIdType.MESH
    used = [0]

    def remote(src, dst, groups=None, band=None, head=None):
        index = used[0]
        used[0] += 1
        return pltpu.make_async_remote_copy(
            src_ref=src,
            dst_ref=dst,
            send_sem=send_sem.at[index],
            recv_sem=recv_sem.at[index],
            device_id=(
                g if groups is None else groups,
                b if band is None else band,
                h if head is None else head,
            ),
            device_id_type=mesh_id,
        )

    opened = []

    def begin(copy, sends=None):
        opened.append((copy, sends))
        if sends is None:
            copy.start()
        else:

            @pl.when(sends)
            def _():
                copy.start()

    def arrive(copy, receives=None):
        if receives is None:
            copy.wait_recv()
        else:

            @pl.when(receives)
            def _():
                copy.wait_recv()

    def channel_rows(shard):
        return pl.ds(pl.multiple_of(shard * local, local), local)

    band_peers = [lax.rem(b + step, bands) for step in range(1, bands)]
    part_peers = [lax.rem(g + step, parts) for step in range(1, parts)]
    mine, crossed, sibs, fars = (channel_rows(s) for s in (h, cross, sibling, far))

    barrier = pltpu.get_barrier_semaphore()
    close = [(g, b, sibling), (g, b, cross), (g, b, far)] + [(peer, b, h) for peer in part_peers]
    for neighbour in close:
        pl.semaphore_signal(barrier, inc=1, device_id=neighbour, device_id_type=mesh_id)

    def tell(sem):
        @pl.when(has_above)
        def _():
            pl.semaphore_signal(sem, inc=1, device_id=(g, above, h), device_id_type=mesh_id)

        @pl.when(has_below)
        def _():
            pl.semaphore_signal(sem, inc=1, device_id=(g, below, h), device_id_type=mesh_id)

    def told(sem, others=0):
        inside = jnp.logical_and(has_above, has_below)

        @pl.when(inside)
        def _():
            pl.semaphore_wait(sem, others + 2)

        @pl.when(jnp.logical_not(inside))
        def _():
            pl.semaphore_wait(sem, others + 1)

    tell(barrier)

    load_lat = pltpu.make_async_copy(lat_hbm, raw_in.at[pl.ds(1, rows), mine, :], local_sem.at[0])
    load_lat.start()
    held_vectors = (vector_0, vector_1, vector_2, vector_3, vector_4, vector_5)
    vectors = (gain_a, shift_a, gain_b, shift_b, bias_a, bias_b)
    load_vectors = [
        pltpu.make_async_copy(vector, held, local_sem.at[4 + index])
        for index, (vector, held) in enumerate(zip(vectors, held_vectors))
    ]
    for load in load_vectors:
        load.start()
    load_kernel = pltpu.make_async_copy(kw_hbm, kw, local_sem.at[1])
    load_rows = pltpu.make_async_copy(pj_hbm, pw.at[:, channel_rows(b), :], local_sem.at[2])
    load_output = pltpu.make_async_copy(ow_hbm, ow, local_sem.at[3])
    load_kernel.start()
    load_rows.start()
    load_output.start()

    count = rows * width * group_width
    both = 2 * groups_here
    sub16 = lax.broadcasted_iota(jnp.int32, (both, width), 0)
    lane16 = lax.broadcasted_iota(jnp.int32, (both, width), 1)
    sub8 = lax.broadcasted_iota(jnp.int32, (groups_here, width), 0)
    lane8 = lax.broadcasted_iota(jnp.int32, (groups_here, width), 1)

    def statistics(buffer, first):
        values = [
            buffer[first + row, mine, :].astype(jnp.float32).reshape(groups_here, group_width, width)
            for row in range(rows)
        ]
        total = sum(jnp.sum(value, axis=1) for value in values)
        mean = jnp.sum(total, axis=1, keepdims=True) / count
        mean = jnp.broadcast_to(mean, (groups_here, width))
        squares = 0.0
        for value in values:
            centered = value - mean[:, None, :]
            squares = squares + jnp.sum(centered * centered, axis=1)
        squares = jnp.broadcast_to(jnp.sum(squares, axis=1, keepdims=True), (groups_here, width))
        stacked = jnp.concatenate([mean, squares], axis=0)
        return jnp.sum(jnp.where(sub16 == lane16, stacked, 0.0), axis=0, keepdims=True)

    def combined(stat):
        found = []
        for shard in (h, sibling, cross, far):
            pieces = [stat[band * heads + shard] for band in range(bands)]
            total = sum(pieces)
            mean = total / bands
            offsets = sum((piece - mean) * (piece - mean) for piece in pieces)
            spread = pltpu.roll(jnp.broadcast_to(total, (8, width)), width - groups_here, 1)[:1]
            scale = lax.rsqrt((spread + offsets * count) / (count * bands) + 1e-05)
            pair_of = []
            for line in (mean, scale):
                wide = jnp.broadcast_to(line, (groups_here, width))
                column = jnp.sum(jnp.where(sub8 == lane8, wide, 0.0), axis=1, keepdims=True)
                pair_of.append(jnp.broadcast_to(column, (groups_here, width)))
            found.append(pair_of)
        return found

    def normalized(value, stats, which, span):
        mean, scale = stats
        grouped = value.astype(jnp.float32).reshape(groups_here, group_width, width)
        scaled = (grouped - mean[:, None, :]) * scale[:, None, :]
        return scaled.reshape(local, width) * spread_par[2 * which, span, :] + spread_par[
            2 * which + 1, span, :
        ]

    load_lat.wait()
    stat_a[b * heads + h] = statistics(raw_in, 1)
    for index, load in enumerate(load_vectors):
        load.wait()
        par[h, index] = held_vectors[index][...].reshape(1, local)

    told(barrier, len(close))

    def gather_pieces(buffer, pieces):
        sent = []
        for piece in pieces:
            own = buffer.at[piece, mine, :]
            there = buffer.at[piece, crossed, :]
            sent.append(
                (
                    remote(own, own, head=cross),
                    remote(own, own, head=sibling),
                    remote(there, there, head=sibling),
                )
            )
        return sent

    own_row = stat_a.at[b * heads + h]
    near_stats = [remote(own_row, own_row, head=peer) for peer in (cross, far, sibling)]
    near_par = [
        remote(par.at[h, pl.ds(0, 4)], par.at[h, pl.ds(0, 4)], head=peer)
        for peer in (cross, far, sibling)
    ]
    edges = (pl.ds(rows, 1), pl.ds(1, 1), pl.ds(2, rows - 2))
    gathered = gather_pieces(raw_in, edges)
    halo = []
    for source, target, peer, sends, receives in (
        (rows, 0, below, has_below, has_above),
        (1, rows + 1, above, has_above, has_below),
    ):
        for shard in (mine, crossed):
            move = remote(raw_in.at[source, shard, :], raw_in.at[target, shard, :], band=peer)
            onward = raw_in.at[target, shard, :]
            halo.append((move, remote(onward, onward, head=sibling), sends, receives))
    for copy in near_stats:
        begin(copy)
    for copy in near_par:
        begin(copy)
    tell(entry_sem.at[0])
    for to_cross, to_sibling, _ in gathered:
        begin(to_cross)
        begin(to_sibling)
    for index in (0, 2):
        move, _, sends, _ = halo[index]
        begin(move, sends)

    share = local // parts

    def share_rows(band, part):
        return pl.ds(pl.multiple_of(band * local + part * share, share), share)

    hops = []
    passed = []
    for kind in range(3):
        steps = []
        for hop in range(1, bands):
            two = []
            for sign, peer in ((1, below), (-1, above)):
                held = lax.rem(b - sign * (hop - 1) + bands, bands)
                got = lax.rem(b - sign * hop + bands, bands)
                if sign > 0:
                    sends = jnp.logical_and(b < bands - 1, b >= hop - 1)
                    receives = b >= hop
                else:
                    sends = jnp.logical_and(b > 0, b + hop - 1 < bands)
                    receives = b + hop < bands
                if hop == 1:
                    source = pj_hbm.at[kind, pl.ds(pl.multiple_of(g * share, share), share), :]
                else:
                    source = pw.at[kind, share_rows(held, g), :]
                move = remote(source, pw.at[kind, share_rows(held, g), :], band=peer)
                two.append((move, sends, receives, got))
            steps.append(two)
        hops.append(steps)
        passed.append([])

    def send_hop(kind, index):
        for move, sends, _, _ in hops[kind][index]:
            begin(move, sends)

    def take_hop(kind, index):
        for move, _, receives, _ in hops[kind][index]:
            arrive(move, receives)
        if index + 1 < len(hops[kind]):
            send_hop(kind, index + 1)
        for _, _, receives, got in hops[kind][index]:
            onward = pw.at[kind, share_rows(got, g), :]
            for peer in part_peers:
                move = remote(onward, onward, groups=peer)
                begin(move, receives)
                passed[kind].append((move, receives))

    plan = {'bs': '+K0', 'G': '+V0 +Q0 -K0', 'H1': '-V0', 'mid': '-Q0 -K1', 'T': '-V1 -Q1', 'T2': '-K2', 'R0': '-V2', 'R1': '-Q2'}

    def go(point):
        for word in plan.get(point, "").split():
            kind, index = "QKV".index(word[1]), int(word[2])
            if word[0] == "+":
                send_hop(kind, index)
            else:
                take_hop(kind, index)

    for copy in near_stats:
        arrive(copy)
    told(entry_sem.at[0])
    tell(entry_sem.at[1])
    told(entry_sem.at[1])
    block = stat_a.at[pl.ds(b * heads, heads)]
    band_stats = [remote(block, block, band=peer) for peer in band_peers]
    for copy in band_stats:
        begin(copy)
    go('bs')

    for copy in near_par:
        arrive(copy)
    blocks = -(-local // width)
    lines = []
    for shard in range(heads):
        for index in range(4):
            lines.append(par[shard, index])
    lines += [par[h, 4], par[h, 5]]
    gap = jnp.zeros((1, blocks * width - local), jnp.float32)
    flat = []
    for line in lines:
        line = jnp.concatenate([line, gap], axis=1)
        flat += [line[:, k * width : (k + 1) * width] for k in range(blocks)]
    flat.append(jnp.zeros((-len(flat) % width, width), jnp.float32))
    columns = jnp.concatenate(flat, axis=0).T

    def column(index):
        pieces = [columns[:, index * blocks + k : index * blocks + k + 1] for k in range(blocks)]
        return jnp.broadcast_to(jnp.concatenate(pieces, axis=0)[:local], (local, width))

    for index in range(4):
        for shard in range(heads):
            spread_par[index, shard * local : (shard + 1) * local, :] = column(shard * 4 + index)
    for index in range(2):
        spread_par[4 + index, :local, :] = column(heads * 4 + index)

    for index in range(2):
        to_cross, _, onward = gathered[index]
        arrive(to_cross)
        begin(onward)
        move, _, sends, _ = halo[2 * index + 1]
        begin(move, sends)
    for index in (0, 2):
        move, onward, _, receives = halo[index]
        arrive(move, receives)
        begin(onward, receives)
    for target, receives in ((0, has_above), (rows + 1, has_below)):

        @pl.when(jnp.logical_not(receives))
        def _(target=target):
            grid_in[target] = jnp.zeros((channels, width), jnp.bfloat16)

    go('G')
    to_cross, _, onward = gathered[2]
    arrive(to_cross)
    begin(onward)
    for copy in band_stats:
        arrive(copy)
    first = combined(stat_a)

    def activate(row, slot, span):
        value = 0.5 * normalized(raw_in[row, span, :], first[slot], 0, span)
        grid_in[row, span, :] = (value + value * jnp.tanh(value)).astype(jnp.bfloat16)

    def activate_edge(target, receives, slots):
        @pl.when(receives)
        def _():
            for slot, span in slots:
                activate(target, slot, span)

    def half(which):
        return pl.ds(pl.multiple_of(which * pair, pair), pair)

    def convolve(which, overs, fresh):
        span = half(which)
        total = None
        for over in overs:
            window = jnp.concatenate([grid_in[over + row, span, :] for row in range(rows)], axis=1)
            weights = kw[over, :, :, span].reshape(3 * local, pair)
            part = jnp.dot(weights, window, preferred_element_type=jnp.float32)
            total = part if total is None else total + part
        if not fresh:
            total = sums[...] + total
        sums[...] = total

    this_half, other_half = h // 2, cross // 2
    near_slots = ((0, mine), (1, sibs))
    far_slots = ((2, crossed), (3, fars))
    for _, to_sibling, _ in gathered:
        arrive(to_sibling)
    for row in range(rows):
        for slot, span in near_slots:
            activate(1 + row, slot, span)
    go('C')
    load_kernel.wait()
    convolve(this_half, (1,), True)
    for index in (0, 2):
        _, onward, _, receives = halo[index]
        arrive(onward, receives)
    activate_edge(0, has_above, near_slots)
    activate_edge(rows + 1, has_below, near_slots)
    for index in (1, 3):
        move, onward, _, receives = halo[index]
        arrive(move, receives)
        begin(onward, receives)
    convolve(this_half, (0, 2), False)
    go('H1')
    for _, _, onward in gathered:
        arrive(onward)
    for row in range(rows):
        for slot, span in far_slots:
            activate(1 + row, slot, span)
    convolve(other_half, (1,), False)
    for index in (1, 3):
        _, onward, _, receives = halo[index]
        arrive(onward, receives)
    activate_edge(0, has_above, far_slots)
    activate_edge(rows + 1, has_below, far_slots)
    go('mid')
    convolve(other_half, (0, 2), False)

    place = lax.broadcasted_iota(jnp.int32, (local, width), 1)
    normed = gather_pieces(conv_in, tuple(pl.ds(row, 1) for row in range(rows)))
    for row in range(rows):
        span = slice(row * width, (row + 1) * width)
        left = jnp.where(place == 0, 0.0, pltpu.roll(sums[:local, span], 1, 1))
        right = jnp.where(place == width - 1, 0.0, pltpu.roll(sums[2 * local :, span], width - 1, 1))
        value = (
            raw_in[1 + row, mine, :].astype(jnp.float32)
            + spread_par[4, :local, :]
            + (sums[local : 2 * local, span] + left + right)
        )
        conv_in[row, mine, :] = value.astype(jnp.bfloat16)
        wide_ref[row] = value.astype(jnp.bfloat16)

    stat_b[b * heads + h] = statistics(conv_in, 0)
    own_row = stat_b.at[b * heads + h]
    all_stats = [
        remote(own_row, own_row, band=lax.rem(b + up, bands), head=lax.rem(h + over, heads))
        for up in range(bands - 1, -1, -1)
        for over in range(heads - 1, -1, -1)
        if up or over
    ]
    for copy in all_stats:
        begin(copy)
    for row in range(rows):
        begin(normed[row][0])
        begin(normed[row][1])
    load_rows.wait()
    go('T')
    arrive(normed[0][0])
    begin(normed[0][2])
    go('T2')
    for copy in all_stats:
        arrive(copy)
    second = combined(stat_b)
    arrive(normed[1][0])
    begin(normed[1][2])
    go('T3')
    for move, receives in passed[1]:
        arrive(move, receives)

    def normalize_row(row):
        arrive(normed[row][1])
        span = slice(row * width, (row + 1) * width)
        for slot, shard in ((0, mine), (1, sibs), (2, crossed)):
            feats[shard, span] = normalized(conv_in[row, shard, :], second[slot], 1, shard).astype(
                jnp.bfloat16
            )
        arrive(normed[row][2])
        feats[fars, span] = normalized(conv_in[row, fars, :], second[3], 1, fars).astype(jnp.bfloat16)

    def project(kind, span):
        return jnp.dot(turned[kind], feats[:, span], preferred_element_type=jnp.float32).astype(
            jnp.bfloat16
        )

    def place_heads(kind, made, chosen):
        for head in range(bands):
            for index, row in enumerate(chosen):
                qkv_out[kind, head, row] = made[
                    head * HEAD_SIZE : (head + 1) * HEAD_SIZE, index * width : (index + 1) * width
                ]

    def spread_rows(kind, row, size):
        chosen = pl.ds(row, size)
        qkv_in[kind, b, chosen] = qkv_out[kind, b, chosen]
        moves = [
            remote(qkv_out.at[kind, peer, chosen], qkv_in.at[kind, b, chosen], band=peer)
            for peer in band_peers
        ]
        for copy in moves:
            begin(copy)
        return moves

    turned[1] = pw[1].T
    moved_keys = []
    for row in range(rows):
        normalize_row(row)
        if row + 2 < rows:
            arrive(normed[row + 2][0])
            begin(normed[row + 2][2])
        place_heads(1, project(1, slice(row * width, (row + 1) * width)), (row,))
        moved_keys += spread_rows(1, row, 1)
        go('R%d' % row)
    go('RE')
    everything = slice(0, tokens)
    for move, receives in passed[2]:
        arrive(move, receives)
    turned[2] = pw[2].T
    place_heads(2, project(2, everything), range(rows))
    moved_values = spread_rows(2, 0, rows)
    for move, receives in passed[0]:
        arrive(move, receives)
    turned[0] = pw[0].T
    place_heads(0, project(0, everything), range(rows))
    moved_queries = [spread_rows(0, row, 1) for row in range(rows)]

    inner = bands * HEAD_SIZE
    factor = HEAD_SIZE ** (-0.5) * math.log2(math.e)

    def feature_rows(shard):
        return pl.ds(pl.multiple_of(shard * inner, inner), inner)

    own_features = pl.ds(pl.multiple_of(h * inner + b * HEAD_SIZE, HEAD_SIZE), HEAD_SIZE)
    returned = [
        [
            remote(att_out.at[row, peer], att_in.at[row, own_features, :], band=peer)
            for peer in band_peers
        ]
        for row in range(rows)
    ]
    final = []
    for row in range(rows):
        own = att_in.at[row, feature_rows(h), :]
        there = att_in.at[row, feature_rows(cross), :]
        final.append(
            (
                remote(own, own, head=cross),
                remote(own, own, head=sibling),
                remote(there, there, head=sibling),
            )
        )

    def pass_on(row):
        for copy in returned[row]:
            arrive(copy)
        begin(final[row][0])
        begin(final[row][1])

    def relay(row):
        arrive(final[row][0])
        begin(final[row][2])

    def finish(row):
        arrive(final[row][1])
        arrive(final[row][2])
        outgoing = jnp.dot(ow[...], att_in[row], preferred_element_type=jnp.float32)
        gain_ref[row] = (
            conv_in[row, mine, :].astype(jnp.float32) + spread_par[5, :local, :] + outgoing
        ).astype(jnp.bfloat16)

    for copy in moved_keys:
        arrive(copy)
    keys = jnp.concatenate(
        [qkv_in[1, source, row] for source in range(bands) for row in range(rows)], axis=1
    ).T
    for copy in moved_values:
        arrive(copy)
    values = jnp.concatenate(
        [qkv_in[2, source, row] for source in range(bands) for row in range(rows)], axis=1
    )
    for row in range(rows):
        for copy in moved_queries[row]:
            arrive(copy)
        query = jnp.concatenate([qkv_in[0, source, row] for source in range(bands)], axis=1)
        scores = jnp.dot(keys, query, preferred_element_type=jnp.float32)
        top = jnp.max(scores, axis=0, keepdims=True)
        heavy = jnp.exp2((scores - top) * factor)
        total = jnp.sum(heavy, axis=0, keepdims=True)
        mixed = jnp.dot(values, heavy.astype(jnp.bfloat16), preferred_element_type=jnp.float32)
        result = (mixed / total).astype(jnp.bfloat16)
        for source in range(bands):
            att_out[row, source] = result[:, source * width : (source + 1) * width]
        for copy in returned[row]:
            begin(copy)
        att_in[row, own_features, :] = att_out[row, b]
        if row >= 1:
            pass_on(row - 1)
        if row >= 2:
            relay(row - 2)
    load_output.wait()
    pass_on(rows - 1)
    if rows >= 2:
        relay(rows - 2)
    for row in range(rows - 1):
        finish(row)
    relay(rows - 1)
    finish(rows - 1)

    for copy, sends in opened:
        if sends is None:
            copy.wait_send()
        else:

            @pl.when(sends)
            def _(copy=copy):
                copy.wait_send()


def pair_shards(
    parts,
    bands,
    heads,
    latent,
    first_gain,
    first_shift,
    kernel,
    kernel_bias,
    second_gain,
    second_shift,
    projection,
    output_weight,
    output_bias,
):
    rows, width, local = latent.shape
    channels, tokens = local * heads, rows * width
    inner = projection.shape[2]
    vectors = [first_gain, first_shift, second_gain, second_shift, kernel_bias, output_bias]
    vmem = pl.BlockSpec(memory_space=pltpu.VMEM)
    hbm = pl.BlockSpec(memory_space=pl.ANY)
    result = jax.ShapeDtypeStruct((rows, local, width), jnp.bfloat16)
    copies = 160
    call = pl.pallas_call(
        functools.partial(pair_kernel, (parts, bands, heads, rows, local, width)),
        out_shape=(result, result),
        in_specs=[hbm] * 10,
        out_specs=(vmem, vmem),
        scratch_shapes=[
            pltpu.VMEM((3, 3, local, channels), jnp.bfloat16),
            pltpu.VMEM((3, channels, inner), jnp.bfloat16),
            pltpu.VMEM((3, inner, channels), jnp.bfloat16),
            pltpu.VMEM((local, inner * heads), jnp.bfloat16),
            pltpu.VMEM((heads, 6, 1, local), jnp.float32),
            pltpu.VMEM((6, channels, width), jnp.float32),
            pltpu.VMEM((bands * heads, 1, width), jnp.float32),
            pltpu.VMEM((bands * heads, 1, width), jnp.float32),
            pltpu.VMEM((rows + 2, channels, width), jnp.bfloat16),
            pltpu.VMEM((rows + 2, channels, width), jnp.bfloat16),
            pltpu.VMEM((3 * local, tokens), jnp.float32),
            pltpu.VMEM((rows, channels, width), jnp.bfloat16),
            pltpu.VMEM((channels, tokens), jnp.bfloat16),
            pltpu.VMEM((3, bands, rows, HEAD_SIZE, width), jnp.bfloat16),
            pltpu.VMEM((3, bands, rows, HEAD_SIZE, width), jnp.bfloat16),
            pltpu.VMEM((rows, bands, HEAD_SIZE, width), jnp.bfloat16),
            pltpu.VMEM((rows, inner * heads, width), jnp.bfloat16),
        ]
        + [pltpu.VMEM((local,), jnp.float32)] * 6
        + [
            pltpu.SemaphoreType.DMA((10,)),
            pltpu.SemaphoreType.REGULAR((2,)),
            pltpu.SemaphoreType.DMA((copies,)),
            pltpu.SemaphoreType.DMA((copies,)),
        ],
        compiler_params=pltpu.CompilerParams(
            collective_id=0, has_side_effects=True, vmem_limit_bytes=60 << 20
        ),
    )
    wide, gained = call(
        jnp.transpose(latent, (0, 2, 1)),
        *vectors,
        jnp.transpose(kernel, (1, 2, 0, 3)),
        jnp.transpose(projection, (1, 0, 2)),
        output_weight,
    )
    top = jnp.finfo(jnp.bfloat16).max
    return tuple(jnp.minimum(jnp.transpose(made, (0, 2, 1)), top) for made in (wide, gained))


def solution(mesh):
    placed = (
        P(("groups", "band"), None, "head"),
        P("head"),
        P("head"),
        P("head", None, None, None),
        P("head"),
        P("head"),
        P("head"),
        P("band", None, "head"),
        P("head", None),
        P("head"),
    )
    parts, bands, heads = (mesh.shape[axis] for axis in ("groups", "band", "head"))
    paired = heads == 4 and bands > 1 and HEADS == heads * bands and CHANNELS % (16 * parts * heads) == 0
    body = functools.partial(pair_shards, parts, bands, heads) if paired else shards
    return jax.shard_map(
        body,
        mesh=mesh,
        in_specs=placed,
        out_specs=(P(("groups", "band"), None, "head"), P(("groups", "band"), None, "head")),
        check_vma=False,
    )
```

```python
import functools
import math

import jax
import jax.numpy as jnp
from jax import lax
from jax.experimental import pallas as pl
from jax.experimental.pallas import tpu as pltpu
from jax.sharding import PartitionSpec as P

CHANNELS = 1280
HEADS = 16
HEAD_SIZE = 64
NORM_GROUPS = 32


def padded_2(cells, sides, width):
    for axis, dim in sides:
        count = lax.axis_size(axis)
        ends = count - 1
        head = lax.slice_in_dim(cells, 0, width, axis=dim)
        tail = lax.slice_in_dim(cells, cells.shape[dim] - width, cells.shape[dim], axis=dim)
        cells = jnp.concatenate(
            [
                lax.ppermute(tail, axis, [(i, (i + 1) % count) for i in range(ends)]),
                cells,
                lax.ppermute(head, axis, [((i + 1) % count, i) for i in range(ends)]),
            ],
            axis=dim,
        )
    return cells


def normalize(values, gain, shift, group_width, count):
    band_rows, width, channels = values.shape
    grouped = values.reshape(band_rows * width, channels // group_width, group_width)
    mean = lax.psum(jnp.sum(grouped, axis=(0, 2)), "band") / count
    centered = grouped - mean[None, :, None]
    spread = lax.psum(jnp.sum(centered * centered, axis=(0, 2)), "band") / count
    scaled = centered * lax.rsqrt(spread + 1e-05)[None, :, None]
    return scaled.reshape(band_rows, width, channels) * gain + shift


def contract_last(left, right):
    return lax.dot_general(
        left, right, (((1,), (1,)), ((), ())), preferred_element_type=jnp.float32
    )


def kernel_block(padded, weights, band_rows, width):
    inputs = padded.shape[2]
    wide = jnp.pad(padded, ((0, 0), (1, 1), (0, 0)))
    summed = jnp.zeros((band_rows * width, weights.shape[0]), jnp.float32)
    for above in range(3):
        for beside in range(3):
            window = wide[above : above + band_rows, beside : beside + width, :].reshape(
                band_rows * width, inputs
            )
            summed = summed + contract_last(window, weights[:, above, beside, :])
    return summed


def shards(
    latent,
    first_gain,
    first_shift,
    kernel,
    kernel_bias,
    second_gain,
    second_shift,
    projection,
    output_weight,
    output_bias,
):
    band_rows, width, channels = latent.shape
    tokens = band_rows * width
    group_width = CHANNELS // NORM_GROUPS
    count = lax.axis_size("band") * band_rows * width * group_width
    outputs = kernel.shape[0]
    latent_wide = latent.astype(jnp.float32)
    activated = jax.nn.silu(
        normalize(latent_wide, first_gain, first_shift, group_width, count)
    ).astype(jnp.bfloat16)
    gathered = lax.all_gather(activated, "head", axis=2, tiled=True)
    padded = padded_2(gathered, (("band", 0),), 1)
    summed = kernel_block(padded, kernel, band_rows, width)
    convolved = (latent_wide + kernel_bias + summed.reshape(band_rows, width, outputs)).astype(
        jnp.bfloat16
    )
    normed = normalize(
        convolved.astype(jnp.float32), second_gain, second_shift, group_width, count
    ).astype(jnp.bfloat16)
    features = lax.all_gather(normed, "head", axis=2, tiled=True).reshape(tokens, CHANNELS)
    local_inner = projection.shape[2]
    local_heads = local_inner // HEAD_SIZE
    piece = lax.all_gather(projection, "band", axis=0, tiled=True)
    projected = jnp.dot(
        features, piece.reshape(piece.shape[0], 3 * local_inner), preferred_element_type=jnp.float32
    )
    projected = projected.astype(jnp.bfloat16).reshape(tokens, 3, local_inner)
    query = projected[:, 0].reshape(tokens, local_heads, HEAD_SIZE)
    key_value = projected[:, 1:]
    factor = HEAD_SIZE ** (-0.5)
    piece = lax.all_gather(key_value, "band", axis=0, tiled=True)
    running = jnp.full((local_heads, tokens), -1e30, jnp.float32)
    keys = piece[:, 0].reshape(piece.shape[0], local_heads, HEAD_SIZE)
    values = piece[:, 1].reshape(piece.shape[0], local_heads, HEAD_SIZE)
    scores = jnp.einsum("qhd,khd->hqk", query, keys, preferred_element_type=jnp.float32) * factor
    highest = jnp.maximum(running, jnp.max(scores, axis=2))
    weights = jnp.exp(scores - highest[:, :, None])
    total = jnp.sum(weights, axis=2)
    summed_values = jnp.einsum(
        "hqk,khd->hqd", weights.astype(jnp.bfloat16), values, preferred_element_type=jnp.float32
    )
    running, total, summed_values = (highest, total, summed_values)
    attention = (
        jnp.transpose(summed_values / total[:, :, None], (1, 0, 2))
        .reshape(tokens, local_inner)
        .astype(jnp.bfloat16)
    )
    outgoing = contract_last(lax.all_gather(attention, "head", axis=1, tiled=True), output_weight)
    attended = (
        convolved.astype(jnp.float32) + output_bias + outgoing.reshape(band_rows, width, outputs)
    )
    return (convolved, attended.astype(jnp.bfloat16))


def pair_kernel(
    shape,
    lat_hbm,
    gain_a,
    shift_a,
    gain_b,
    shift_b,
    bias_a,
    bias_b,
    kw_hbm,
    pj_hbm,
    ow_hbm,
    wide_ref,
    gain_ref,
    kw,
    pw,
    turned,
    ow,
    par,
    spread_par,
    stat_a,
    stat_b,
    raw_in,
    grid_in,
    sums,
    conv_in,
    feats,
    qkv_out,
    qkv_in,
    att_out,
    att_in,
    vector_0,
    vector_1,
    vector_2,
    vector_3,
    vector_4,
    vector_5,
    local_sem,
    entry_sem,
    send_sem,
    recv_sem,
):
    parts, bands, heads, rows, local, width = shape
    channels = local * heads
    tokens = rows * width
    group_width = CHANNELS // NORM_GROUPS
    groups_here = local // group_width
    pair = 2 * local
    g, b, h = lax.axis_index("groups"), lax.axis_index("band"), lax.axis_index("head")
    sibling = h + 1 - 2 * lax.rem(h, 2)
    cross = lax.rem(h + 2, heads)
    far = lax.rem(sibling + 2, heads)
    has_above, has_below = b > 0, b < bands - 1
    above, below = lax.rem(b + bands - 1, bands), lax.rem(b + 1, bands)
    mesh_id = pl.DeviceIdType.MESH
    used = [0]

    def remote(src, dst, groups=None, band=None, head=None):
        index = used[0]
        used[0] += 1
        return pltpu.make_async_remote_copy(
            src_ref=src,
            dst_ref=dst,
            send_sem=send_sem.at[index],
            recv_sem=recv_sem.at[index],
            device_id=(
                g if groups is None else groups,
                b if band is None else band,
                h if head is None else head,
            ),
            device_id_type=mesh_id,
        )

    opened = []

    def begin(copy, sends=None):
        opened.append((copy, sends))
        if sends is None:
            copy.start()
        else:

            @pl.when(sends)
            def _():
                copy.start()

    def arrive(copy, receives=None):
        if receives is None:
            copy.wait_recv()
        else:

            @pl.when(receives)
            def _():
                copy.wait_recv()

    def channel_rows(shard):
        return pl.ds(pl.multiple_of(shard * local, local), local)

    band_peers = [lax.rem(b + 2, bands), bands - 1 - b, b + 1 - 2 * lax.rem(b, 2)]
    part_peers = [lax.rem(g + step, parts) for step in range(1, parts)]
    mine, crossed, sibs, fars = (channel_rows(s) for s in (h, cross, sibling, far))

    barrier = pltpu.get_barrier_semaphore()
    close = [(g, b, sibling), (g, b, cross), (g, b, far)] + [(peer, b, h) for peer in part_peers]
    for neighbour in close:
        pl.semaphore_signal(barrier, inc=1, device_id=neighbour, device_id_type=mesh_id)

    def tell(sem):
        @pl.when(has_above)
        def _():
            pl.semaphore_signal(sem, inc=1, device_id=(g, above, h), device_id_type=mesh_id)

        @pl.when(has_below)
        def _():
            pl.semaphore_signal(sem, inc=1, device_id=(g, below, h), device_id_type=mesh_id)

    def told(sem, others=0):
        inside = jnp.logical_and(has_above, has_below)

        @pl.when(inside)
        def _():
            pl.semaphore_wait(sem, others + 2)

        @pl.when(jnp.logical_not(inside))
        def _():
            pl.semaphore_wait(sem, others + 1)

    tell(barrier)

    load_lat = pltpu.make_async_copy(lat_hbm, raw_in.at[pl.ds(1, rows), mine, :], local_sem.at[0])
    load_lat.start()
    held_vectors = (vector_0, vector_1, vector_2, vector_3, vector_4, vector_5)
    vectors = (gain_a, shift_a, gain_b, shift_b, bias_a, bias_b)
    load_vectors = [
        pltpu.make_async_copy(vector, held, local_sem.at[4 + index])
        for index, (vector, held) in enumerate(zip(vectors, held_vectors))
    ]
    for load in load_vectors:
        load.start()
    load_kernel = pltpu.make_async_copy(kw_hbm, kw, local_sem.at[1])
    load_rows = pltpu.make_async_copy(pj_hbm, pw.at[:, channel_rows(b), :], local_sem.at[2])
    load_output = pltpu.make_async_copy(ow_hbm, ow, local_sem.at[3])
    load_kernel.start()
    load_rows.start()
    load_output.start()

    count = rows * width * group_width
    both = 2 * groups_here
    sub16 = lax.broadcasted_iota(jnp.int32, (both, width), 0)
    lane16 = lax.broadcasted_iota(jnp.int32, (both, width), 1)
    sub8 = lax.broadcasted_iota(jnp.int32, (groups_here, width), 0)
    lane8 = lax.broadcasted_iota(jnp.int32, (groups_here, width), 1)

    def statistics(buffer, first):
        values = [
            buffer[first + row, mine, :].astype(jnp.float32).reshape(groups_here, group_width, width)
            for row in range(rows)
        ]
        total = sum(jnp.sum(value, axis=1) for value in values)
        mean = jnp.sum(total, axis=1, keepdims=True) / count
        mean = jnp.broadcast_to(mean, (groups_here, width))
        squares = 0.0
        for value in values:
            centered = value - mean[:, None, :]
            squares = squares + jnp.sum(centered * centered, axis=1)
        squares = jnp.broadcast_to(jnp.sum(squares, axis=1, keepdims=True), (groups_here, width))
        stacked = jnp.concatenate([mean, squares], axis=0)
        return jnp.sum(jnp.where(sub16 == lane16, stacked, 0.0), axis=0, keepdims=True)

    def combined(stat):
        found = []
        for shard in (h, sibling, cross, far):
            pieces = [stat[band * heads + shard] for band in range(bands)]
            total = sum(pieces)
            mean = total / bands
            offsets = sum((piece - mean) * (piece - mean) for piece in pieces)
            spread = pltpu.roll(jnp.broadcast_to(total, (8, width)), width - groups_here, 1)[:1]
            scale = lax.rsqrt((spread + offsets * count) / (count * bands) + 1e-05)
            pair_of = []
            for line in (mean, scale):
                wide = jnp.broadcast_to(line, (groups_here, width))
                column = jnp.sum(jnp.where(sub8 == lane8, wide, 0.0), axis=1, keepdims=True)
                pair_of.append(jnp.broadcast_to(column, (groups_here, width)))
            found.append(pair_of)
        return found

    def normalized(value, stats, which, span):
        mean, scale = stats
        grouped = value.astype(jnp.float32).reshape(groups_here, group_width, width)
        scaled = (grouped - mean[:, None, :]) * scale[:, None, :]
        return scaled.reshape(local, width) * spread_par[2 * which, span, :] + spread_par[
            2 * which + 1, span, :
        ]

    load_lat.wait()
    stat_a[b * heads + h] = statistics(raw_in, 1)
    for index, load in enumerate(load_vectors):
        load.wait()
        par[h, index] = held_vectors[index][...].reshape(1, local)

    told(barrier, len(close))

    def gather_pieces(buffer, pieces):
        sent = []
        for piece in pieces:
            own = buffer.at[piece, mine, :]
            there = buffer.at[piece, crossed, :]
            sent.append(
                (
                    remote(own, own, head=cross),
                    remote(own, own, head=sibling),
                    remote(there, there, head=sibling),
                )
            )
        return sent

    own_row = stat_a.at[b * heads + h]
    near_stats = [remote(own_row, own_row, head=peer) for peer in (cross, far, sibling)]
    near_par = [
        remote(par.at[h, pl.ds(0, 4)], par.at[h, pl.ds(0, 4)], head=peer)
        for peer in (cross, far, sibling)
    ]
    edges = (pl.ds(rows, 1), pl.ds(1, 1), pl.ds(2, rows - 2))
    gathered = gather_pieces(raw_in, edges)
    halo = []
    for source, target, peer, sends, receives in (
        (rows, 0, below, has_below, has_above),
        (1, rows + 1, above, has_above, has_below),
    ):
        for shard in (mine, crossed):
            move = remote(raw_in.at[source, shard, :], raw_in.at[target, shard, :], band=peer)
            onward = raw_in.at[target, shard, :]
            halo.append((move, remote(onward, onward, head=sibling), sends, receives))
    for copy in near_stats:
        begin(copy)
    for copy in near_par:
        begin(copy)
    tell(entry_sem.at[0])
    for to_cross, to_sibling, _ in gathered:
        begin(to_cross)
        begin(to_sibling)
    for index in (0, 2):
        move, _, sends, _ = halo[index]
        begin(move, sends)

    share = local // parts

    def share_rows(band, part):
        return pl.ds(pl.multiple_of(band * local + part * share, share), share)

    hops = []
    passed = []
    for kind in range(3):
        steps = []
        for hop in range(1, bands):
            two = []
            for sign, peer in ((1, below), (-1, above)):
                held = lax.rem(b - sign * (hop - 1) + bands, bands)
                got = lax.rem(b - sign * hop + bands, bands)
                if sign > 0:
                    sends = jnp.logical_and(b < bands - 1, b >= hop - 1)
                    receives = b >= hop
                else:
                    sends = jnp.logical_and(b > 0, b + hop - 1 < bands)
                    receives = b + hop < bands
                if hop == 1:
                    source = pj_hbm.at[kind, pl.ds(pl.multiple_of(g * share, share), share), :]
                else:
                    source = pw.at[kind, share_rows(held, g), :]
                move = remote(source, pw.at[kind, share_rows(held, g), :], band=peer)
                two.append((move, sends, receives, got))
            steps.append(two)
        hops.append(steps)
        passed.append([])

    def send_hop(kind, index):
        for move, sends, _, _ in hops[kind][index]:
            begin(move, sends)

    def take_hop(kind, index):
        for move, _, receives, _ in hops[kind][index]:
            arrive(move, receives)
        if index + 1 < len(hops[kind]):
            send_hop(kind, index + 1)
        for _, _, receives, got in hops[kind][index]:
            onward = pw.at[kind, share_rows(got, g), :]
            for peer in part_peers:
                move = remote(onward, onward, groups=peer)
                begin(move, receives)
                passed[kind].append((move, receives))

    plan = {'bs': '+K0', 'G': '+V0 +Q0 -K0', 'H1': '-V0', 'mid': '-Q0 -K1', 'T': '-V1 -Q1', 'T2': '-K2', 'R0': '-V2', 'R1': '-Q2'}

    def go(point):
        for word in plan.get(point, "").split():
            kind, index = "QKV".index(word[1]), int(word[2])
            if word[0] == "+":
                send_hop(kind, index)
            else:
                take_hop(kind, index)

    for copy in near_stats:
        arrive(copy)
    told(entry_sem.at[0])
    tell(entry_sem.at[1])
    told(entry_sem.at[1])
    block = stat_a.at[pl.ds(b * heads, heads)]
    band_stats = [remote(block, block, band=peer) for peer in band_peers]
    for copy in band_stats:
        begin(copy)
    go('bs')

    for copy in near_par:
        arrive(copy)
    blocks = -(-local // width)
    lines = []
    for shard in range(heads):
        for index in range(4):
            lines.append(par[shard, index])
    lines += [par[h, 4], par[h, 5]]
    gap = jnp.zeros((1, blocks * width - local), jnp.float32)
    flat = []
    for line in lines:
        line = jnp.concatenate([line, gap], axis=1)
        flat += [line[:, k * width : (k + 1) * width] for k in range(blocks)]
    flat.append(jnp.zeros((-len(flat) % width, width), jnp.float32))
    columns = jnp.concatenate(flat, axis=0).T

    def column(index):
        pieces = [columns[:, index * blocks + k : index * blocks + k + 1] for k in range(blocks)]
        return jnp.broadcast_to(jnp.concatenate(pieces, axis=0)[:local], (local, width))

    for index in range(4):
        for shard in range(heads):
            spread_par[index, shard * local : (shard + 1) * local, :] = column(shard * 4 + index)
    for index in range(2):
        spread_par[4 + index, :local, :] = column(heads * 4 + index)

    for index in range(2):
        to_cross, _, onward = gathered[index]
        arrive(to_cross)
        begin(onward)
        move, _, sends, _ = halo[2 * index + 1]
        begin(move, sends)
    for index in (0, 2):
        move, onward, _, receives = halo[index]
        arrive(move, receives)
        begin(onward, receives)
    for target, receives in ((0, has_above), (rows + 1, has_below)):

        @pl.when(jnp.logical_not(receives))
        def _(target=target):
            grid_in[target] = jnp.zeros((channels, width), jnp.bfloat16)

    go('G')
    to_cross, _, onward = gathered[2]
    arrive(to_cross)
    begin(onward)
    for copy in band_stats:
        arrive(copy)
    first = combined(stat_a)

    def activate(row, slot, span):
        value = 0.5 * normalized(raw_in[row, span, :], first[slot], 0, span)
        grid_in[row, span, :] = (value + value * jnp.tanh(value)).astype(jnp.bfloat16)

    def activate_edge(target, receives, slots):
        @pl.when(receives)
        def _():
            for slot, span in slots:
                activate(target, slot, span)

    def half(which):
        return pl.ds(pl.multiple_of(which * pair, pair), pair)

    def convolve(which, overs, fresh, chosen=range(rows)):
        span = half(which)
        place = slice(chosen[0] * width, (chosen[-1] + 1) * width)
        total = None
        for over in overs:
            window = jnp.concatenate([grid_in[over + row, span, :] for row in chosen], axis=1)
            weights = kw[over, :, :, span].reshape(3 * local, pair)
            part = jnp.dot(weights, window, preferred_element_type=jnp.float32)
            total = part if total is None else total + part
        if not fresh:
            total = sums[:, place] + total
        sums[:, place] = total

    this_half, other_half = h // 2, cross // 2
    near_slots = ((0, mine), (1, sibs))
    far_slots = ((2, crossed), (3, fars))
    for _, to_sibling, _ in gathered:
        arrive(to_sibling)
    for row in range(rows):
        for slot, span in near_slots:
            activate(1 + row, slot, span)
    go('C')
    load_kernel.wait()
    convolve(this_half, (1,), True)
    for index in (0, 2):
        _, onward, _, receives = halo[index]
        arrive(onward, receives)
    activate_edge(0, has_above, near_slots)
    activate_edge(rows + 1, has_below, near_slots)
    for index in (1, 3):
        move, onward, _, receives = halo[index]
        arrive(move, receives)
        begin(onward, receives)
    convolve(this_half, (0, 2), False)
    go('H1')
    for _, _, onward in gathered:
        arrive(onward)
    for row in range(rows):
        for slot, span in far_slots:
            activate(1 + row, slot, span)
    convolve(other_half, (1,), False)
    for index in (1, 3):
        _, onward, _, receives = halo[index]
        arrive(onward, receives)
    activate_edge(0, has_above, far_slots)
    activate_edge(rows + 1, has_below, far_slots)
    go('mid')
    place = lax.broadcasted_iota(jnp.int32, (local, width), 1)
    normed = gather_pieces(conv_in, tuple(pl.ds(row, 1) for row in range(rows)))

    def close_row(row):
        span = slice(row * width, (row + 1) * width)
        left = jnp.where(place == 0, 0.0, pltpu.roll(sums[:local, span], 1, 1))
        right = jnp.where(place == width - 1, 0.0, pltpu.roll(sums[2 * local :, span], width - 1, 1))
        value = (
            raw_in[1 + row, mine, :].astype(jnp.float32)
            + spread_par[4, :local, :]
            + (sums[local : 2 * local, span] + left + right)
        )
        conv_in[row, mine, :] = value.astype(jnp.bfloat16)
        wide_ref[row] = value.astype(jnp.bfloat16)

    def send_row(row):
        begin(normed[row][0])
        begin(normed[row][1])

    convolve(other_half, (0, 2), False, range(1))
    close_row(0)
    send_row(0)
    convolve(other_half, (0, 2), False, range(1, rows))
    for row in range(1, rows):
        close_row(row)
    stat_b[b * heads + h] = statistics(conv_in, 0)
    own_row = stat_b.at[b * heads + h]
    all_stats = [
        remote(own_row, own_row, band=lax.rem(b + up, bands), head=lax.rem(h + over, heads))
        for up in range(bands - 1, -1, -1)
        for over in range(heads - 1, -1, -1)
        if up or over
    ]
    for copy in all_stats:
        begin(copy)
    for row in range(1, rows):
        send_row(row)
    load_rows.wait()
    go('T')
    arrive(normed[0][0])
    begin(normed[0][2])
    go('T2')
    for copy in all_stats:
        arrive(copy)
    second = combined(stat_b)
    arrive(normed[1][0])
    begin(normed[1][2])
    go('T3')
    for move, receives in passed[1]:
        arrive(move, receives)

    def normalize_row(row):
        arrive(normed[row][1])
        span = slice(row * width, (row + 1) * width)
        for slot, shard in ((0, mine), (1, sibs), (2, crossed)):
            feats[shard, span] = normalized(conv_in[row, shard, :], second[slot], 1, shard).astype(
                jnp.bfloat16
            )
        arrive(normed[row][2])
        feats[fars, span] = normalized(conv_in[row, fars, :], second[3], 1, fars).astype(jnp.bfloat16)

    def project(kind, span):
        return jnp.dot(turned[kind], feats[:, span], preferred_element_type=jnp.float32).astype(
            jnp.bfloat16
        )

    def place_heads(kind, made, chosen):
        for head in range(bands):
            for index, row in enumerate(chosen):
                qkv_out[kind, head, row] = made[
                    head * HEAD_SIZE : (head + 1) * HEAD_SIZE, index * width : (index + 1) * width
                ]

    def spread_rows(kind, row, size):
        chosen = pl.ds(row, size)
        qkv_in[kind, b, chosen] = qkv_out[kind, b, chosen]
        moves = [
            remote(qkv_out.at[kind, peer, chosen], qkv_in.at[kind, b, chosen], band=peer)
            for peer in band_peers
        ]
        for copy in moves:
            begin(copy)
        return moves

    turned[1] = pw[1].T
    moved_keys = []
    for row in range(rows):
        normalize_row(row)
        if row + 2 < rows:
            arrive(normed[row + 2][0])
            begin(normed[row + 2][2])
        place_heads(1, project(1, slice(row * width, (row + 1) * width)), (row,))
        moved_keys += spread_rows(1, row, 1)
        go('R%d' % row)
    go('RE')
    everything = slice(0, tokens)
    for move, receives in passed[2]:
        arrive(move, receives)
    turned[2] = pw[2].T
    place_heads(2, project(2, everything), range(rows))
    moved_values = spread_rows(2, 0, rows)
    for move, receives in passed[0]:
        arrive(move, receives)
    turned[0] = pw[0].T
    place_heads(0, project(0, everything), range(rows))
    moved_queries = [spread_rows(0, row, 1) for row in range(rows)]

    inner = bands * HEAD_SIZE
    factor = HEAD_SIZE ** (-0.5) * math.log2(math.e)

    def feature_rows(shard):
        return pl.ds(pl.multiple_of(shard * inner, inner), inner)

    own_features = pl.ds(pl.multiple_of(h * inner + b * HEAD_SIZE, HEAD_SIZE), HEAD_SIZE)
    final_row = rows - 1
    returned = [
        [
            remote(att_out.at[row, index], att_in.at[row, own_features, :], band=peer)
            for index, peer in enumerate(band_peers)
        ]
        for row in range(rows)
    ]
    direct = [
        remote(
            att_out.at[final_row, index],
            att_in.at[final_row, own_features, :],
            band=peer,
            head=cross,
        )
        for index, peer in enumerate(band_peers)
    ]
    own_final = att_in.at[final_row, own_features, :]
    direct.append(remote(own_final, own_final, head=cross))
    final = []
    for row in range(rows):
        own = att_in.at[row, feature_rows(h), :]
        there = att_in.at[row, feature_rows(cross), :]
        to_cross = remote(own, own, head=cross) if row < final_row else None
        final.append(
            (to_cross, remote(own, own, head=sibling), remote(there, there, head=sibling))
        )

    def pass_on(row):
        for copy in returned[row]:
            arrive(copy)
        if row < final_row:
            begin(final[row][0])
        begin(final[row][1])

    def relay(row):
        for copy in direct if row == final_row else final[row][:1]:
            arrive(copy)
        begin(final[row][2])

    def finish(row):
        arrive(final[row][1])
        arrive(final[row][2])
        outgoing = jnp.dot(ow[...], att_in[row], preferred_element_type=jnp.float32)
        gain_ref[row] = (
            conv_in[row, mine, :].astype(jnp.float32) + spread_par[5, :local, :] + outgoing
        ).astype(jnp.bfloat16)

    for copy in moved_keys:
        arrive(copy)
    keys = jnp.concatenate(
        [qkv_in[1, source, row] for source in range(bands) for row in range(rows)], axis=1
    ).T
    for copy in moved_values:
        arrive(copy)
    values = jnp.concatenate(
        [qkv_in[2, source, row] for source in range(bands) for row in range(rows)], axis=1
    )

    def attend(pieces):
        query = jnp.concatenate(pieces, axis=1)
        scores = jnp.dot(keys, query, preferred_element_type=jnp.float32)
        top = jnp.max(scores, axis=0, keepdims=True)
        heavy = jnp.exp2((scores - top) * factor)
        total = jnp.sum(heavy, axis=0, keepdims=True)
        mixed = jnp.dot(values, heavy.astype(jnp.bfloat16), preferred_element_type=jnp.float32)
        result = (mixed / total).astype(jnp.bfloat16)
        return [result[:, k * width : (k + 1) * width] for k in range(len(pieces))]

    for row, result in enumerate(attend([qkv_out[0, b, row] for row in range(rows)])):
        att_in[row, own_features, :] = result
    begin(direct[-1])
    for row in range(rows):
        for copy in moved_queries[row]:
            arrive(copy)
        for index, result in enumerate(attend([qkv_in[0, peer, row] for peer in band_peers])):
            att_out[row, index] = result
        for copy in returned[row]:
            begin(copy)
        if row == final_row:
            for copy in direct[:-1]:
                begin(copy)
        if row >= 1:
            pass_on(row - 1)
    load_output.wait()
    relay(0)
    pass_on(final_row)
    for row in range(1, rows):
        relay(row)
    for row in range(rows):
        finish(row)

    for copy, sends in opened:
        if sends is None:
            copy.wait_send()
        else:

            @pl.when(sends)
            def _(copy=copy):
                copy.wait_send()


def pair_shards(
    parts,
    bands,
    heads,
    latent,
    first_gain,
    first_shift,
    kernel,
    kernel_bias,
    second_gain,
    second_shift,
    projection,
    output_weight,
    output_bias,
):
    rows, width, local = latent.shape
    channels, tokens = local * heads, rows * width
    inner = projection.shape[2]
    vectors = [first_gain, first_shift, second_gain, second_shift, kernel_bias, output_bias]
    vmem = pl.BlockSpec(memory_space=pltpu.VMEM)
    hbm = pl.BlockSpec(memory_space=pl.ANY)
    result = jax.ShapeDtypeStruct((rows, local, width), jnp.bfloat16)
    copies = 160
    call = pl.pallas_call(
        functools.partial(pair_kernel, (parts, bands, heads, rows, local, width)),
        out_shape=(result, result),
        in_specs=[hbm] * 10,
        out_specs=(vmem, vmem),
        scratch_shapes=[
            pltpu.VMEM((3, 3, local, channels), jnp.bfloat16),
            pltpu.VMEM((3, channels, inner), jnp.bfloat16),
            pltpu.VMEM((3, inner, channels), jnp.bfloat16),
            pltpu.VMEM((local, inner * heads), jnp.bfloat16),
            pltpu.VMEM((heads, 6, 1, local), jnp.float32),
            pltpu.VMEM((6, channels, width), jnp.float32),
            pltpu.VMEM((bands * heads, 1, width), jnp.float32),
            pltpu.VMEM((bands * heads, 1, width), jnp.float32),
            pltpu.VMEM((rows + 2, channels, width), jnp.bfloat16),
            pltpu.VMEM((rows + 2, channels, width), jnp.bfloat16),
            pltpu.VMEM((3 * local, tokens), jnp.float32),
            pltpu.VMEM((rows, channels, width), jnp.bfloat16),
            pltpu.VMEM((channels, tokens), jnp.bfloat16),
            pltpu.VMEM((3, bands, rows, HEAD_SIZE, width), jnp.bfloat16),
            pltpu.VMEM((3, bands, rows, HEAD_SIZE, width), jnp.bfloat16),
            pltpu.VMEM((rows, bands - 1, HEAD_SIZE, width), jnp.bfloat16),
            pltpu.VMEM((rows, inner * heads, width), jnp.bfloat16),
        ]
        + [pltpu.VMEM((local,), jnp.float32)] * 6
        + [
            pltpu.SemaphoreType.DMA((10,)),
            pltpu.SemaphoreType.REGULAR((2,)),
            pltpu.SemaphoreType.DMA((copies,)),
            pltpu.SemaphoreType.DMA((copies,)),
        ],
        compiler_params=pltpu.CompilerParams(
            collective_id=0, has_side_effects=True, vmem_limit_bytes=60 << 20
        ),
    )
    wide, gained = call(
        jnp.transpose(latent, (0, 2, 1)),
        *vectors,
        jnp.transpose(kernel, (1, 2, 0, 3)),
        jnp.transpose(projection, (1, 0, 2)),
        output_weight,
    )
    top = jnp.finfo(jnp.bfloat16).max
    return tuple(jnp.minimum(jnp.transpose(made, (0, 2, 1)), top) for made in (wide, gained))


def solution(mesh):
    placed = (
        P(("groups", "band"), None, "head"),
        P("head"),
        P("head"),
        P("head", None, None, None),
        P("head"),
        P("head"),
        P("head"),
        P("band", None, "head"),
        P("head", None),
        P("head"),
    )
    parts, bands, heads = (mesh.shape[axis] for axis in ("groups", "band", "head"))
    paired = heads == 4 and bands > 1 and HEADS == heads * bands and CHANNELS % (16 * parts * heads) == 0
    body = functools.partial(pair_shards, parts, bands, heads) if paired else shards
    return jax.shard_map(
        body,
        mesh=mesh,
        in_specs=placed,
        out_specs=(P(("groups", "band"), None, "head"), P(("groups", "band"), None, "head")),
        check_vma=False,
    )
```

```python
import functools
import math

import jax
import jax.numpy as jnp
from jax import lax
from jax.experimental import pallas as pl
from jax.experimental.pallas import tpu as pltpu
from jax.sharding import PartitionSpec as P

CHANNELS = 1280
HEADS = 16
HEAD_SIZE = 64
NORM_GROUPS = 32


def padded_2(cells, sides, width):
    for axis, dim in sides:
        count = lax.axis_size(axis)
        ends = count - 1
        head = lax.slice_in_dim(cells, 0, width, axis=dim)
        tail = lax.slice_in_dim(cells, cells.shape[dim] - width, cells.shape[dim], axis=dim)
        cells = jnp.concatenate(
            [
                lax.ppermute(tail, axis, [(i, (i + 1) % count) for i in range(ends)]),
                cells,
                lax.ppermute(head, axis, [((i + 1) % count, i) for i in range(ends)]),
            ],
            axis=dim,
        )
    return cells


def normalize(values, gain, shift, group_width, count):
    band_rows, width, channels = values.shape
    grouped = values.reshape(band_rows * width, channels // group_width, group_width)
    mean = lax.psum(jnp.sum(grouped, axis=(0, 2)), "band") / count
    centered = grouped - mean[None, :, None]
    spread = lax.psum(jnp.sum(centered * centered, axis=(0, 2)), "band") / count
    scaled = centered * lax.rsqrt(spread + 1e-05)[None, :, None]
    return scaled.reshape(band_rows, width, channels) * gain + shift


def contract_last(left, right):
    return lax.dot_general(
        left, right, (((1,), (1,)), ((), ())), preferred_element_type=jnp.float32
    )


def kernel_block(padded, weights, band_rows, width):
    inputs = padded.shape[2]
    wide = jnp.pad(padded, ((0, 0), (1, 1), (0, 0)))
    summed = jnp.zeros((band_rows * width, weights.shape[0]), jnp.float32)
    for above in range(3):
        for beside in range(3):
            window = wide[above : above + band_rows, beside : beside + width, :].reshape(
                band_rows * width, inputs
            )
            summed = summed + contract_last(window, weights[:, above, beside, :])
    return summed


def shards(
    latent,
    first_gain,
    first_shift,
    kernel,
    kernel_bias,
    second_gain,
    second_shift,
    projection,
    output_weight,
    output_bias,
):
    band_rows, width, channels = latent.shape
    tokens = band_rows * width
    group_width = CHANNELS // NORM_GROUPS
    count = lax.axis_size("band") * band_rows * width * group_width
    outputs = kernel.shape[0]
    latent_wide = latent.astype(jnp.float32)
    activated = jax.nn.silu(
        normalize(latent_wide, first_gain, first_shift, group_width, count)
    ).astype(jnp.bfloat16)
    gathered = lax.all_gather(activated, "head", axis=2, tiled=True)
    padded = padded_2(gathered, (("band", 0),), 1)
    summed = kernel_block(padded, kernel, band_rows, width)
    convolved = (latent_wide + kernel_bias + summed.reshape(band_rows, width, outputs)).astype(
        jnp.bfloat16
    )
    normed = normalize(
        convolved.astype(jnp.float32), second_gain, second_shift, group_width, count
    ).astype(jnp.bfloat16)
    features = lax.all_gather(normed, "head", axis=2, tiled=True).reshape(tokens, CHANNELS)
    local_inner = projection.shape[2]
    local_heads = local_inner // HEAD_SIZE
    piece = lax.all_gather(projection, "band", axis=0, tiled=True)
    projected = jnp.dot(
        features, piece.reshape(piece.shape[0], 3 * local_inner), preferred_element_type=jnp.float32
    )
    projected = projected.astype(jnp.bfloat16).reshape(tokens, 3, local_inner)
    query = projected[:, 0].reshape(tokens, local_heads, HEAD_SIZE)
    key_value = projected[:, 1:]
    factor = HEAD_SIZE ** (-0.5)
    piece = lax.all_gather(key_value, "band", axis=0, tiled=True)
    running = jnp.full((local_heads, tokens), -1e30, jnp.float32)
    keys = piece[:, 0].reshape(piece.shape[0], local_heads, HEAD_SIZE)
    values = piece[:, 1].reshape(piece.shape[0], local_heads, HEAD_SIZE)
    scores = jnp.einsum("qhd,khd->hqk", query, keys, preferred_element_type=jnp.float32) * factor
    highest = jnp.maximum(running, jnp.max(scores, axis=2))
    weights = jnp.exp(scores - highest[:, :, None])
    total = jnp.sum(weights, axis=2)
    summed_values = jnp.einsum(
        "hqk,khd->hqd", weights.astype(jnp.bfloat16), values, preferred_element_type=jnp.float32
    )
    running, total, summed_values = (highest, total, summed_values)
    attention = (
        jnp.transpose(summed_values / total[:, :, None], (1, 0, 2))
        .reshape(tokens, local_inner)
        .astype(jnp.bfloat16)
    )
    outgoing = contract_last(lax.all_gather(attention, "head", axis=1, tiled=True), output_weight)
    attended = (
        convolved.astype(jnp.float32) + output_bias + outgoing.reshape(band_rows, width, outputs)
    )
    return (convolved, attended.astype(jnp.bfloat16))


def pair_kernel(
    shape,
    lat_hbm,
    gain_a,
    shift_a,
    gain_b,
    shift_b,
    bias_a,
    bias_b,
    kw_hbm,
    pj_hbm,
    ow_hbm,
    wide_ref,
    gain_ref,
    kw,
    pw,
    turned,
    ow,
    par,
    spread_par,
    stat_a,
    stat_b,
    raw_in,
    grid_in,
    sums,
    conv_in,
    feats,
    qkv_out,
    qkv_in,
    att_out,
    att_in,
    vector_0,
    vector_1,
    vector_2,
    vector_3,
    vector_4,
    vector_5,
    local_sem,
    entry_sem,
    send_sem,
    recv_sem,
):
    parts, bands, heads, rows, local, width = shape
    channels = local * heads
    tokens = rows * width
    group_width = CHANNELS // NORM_GROUPS
    groups_here = local // group_width
    pair = 2 * local
    g, b, h = lax.axis_index("groups"), lax.axis_index("band"), lax.axis_index("head")
    sibling = h + 1 - 2 * lax.rem(h, 2)
    cross = lax.rem(h + 2, heads)
    far = lax.rem(sibling + 2, heads)
    has_above, has_below = b > 0, b < bands - 1
    above, below = lax.rem(b + bands - 1, bands), lax.rem(b + 1, bands)
    mesh_id = pl.DeviceIdType.MESH
    used = [0]

    def remote(src, dst, groups=None, band=None, head=None):
        index = used[0]
        used[0] += 1
        return pltpu.make_async_remote_copy(
            src_ref=src,
            dst_ref=dst,
            send_sem=send_sem.at[index],
            recv_sem=recv_sem.at[index],
            device_id=(
                g if groups is None else groups,
                b if band is None else band,
                h if head is None else head,
            ),
            device_id_type=mesh_id,
        )

    opened = []

    def begin(copy, sends=None):
        opened.append((copy, sends))
        if sends is None:
            copy.start()
        else:

            @pl.when(sends)
            def _():
                copy.start()

    settled = [0]

    def settle(until):
        for copy, sends in opened[settled[0] : until]:
            if sends is None:
                copy.wait_send()
            else:

                @pl.when(sends)
                def _(copy=copy):
                    copy.wait_send()

        settled[0] = max(settled[0], until)

    def arrive(copy, receives=None):
        if receives is None:
            copy.wait_recv()
        else:

            @pl.when(receives)
            def _():
                copy.wait_recv()

    def channel_rows(shard):
        return pl.ds(pl.multiple_of(shard * local, local), local)

    band_peers = [lax.rem(b + 2, bands), bands - 1 - b, b + 1 - 2 * lax.rem(b, 2)]
    part_peers = [lax.rem(g + step, parts) for step in range(1, parts)]
    mine, crossed, sibs, fars = (channel_rows(s) for s in (h, cross, sibling, far))

    barrier = pltpu.get_barrier_semaphore()
    close = [(g, b, sibling), (g, b, cross), (g, b, far)] + [(peer, b, h) for peer in part_peers]
    for neighbour in close:
        pl.semaphore_signal(barrier, inc=1, device_id=neighbour, device_id_type=mesh_id)

    def tell(sem):
        @pl.when(has_above)
        def _():
            pl.semaphore_signal(sem, inc=1, device_id=(g, above, h), device_id_type=mesh_id)

        @pl.when(has_below)
        def _():
            pl.semaphore_signal(sem, inc=1, device_id=(g, below, h), device_id_type=mesh_id)

    def told(sem, others=0):
        inside = jnp.logical_and(has_above, has_below)

        @pl.when(inside)
        def _():
            pl.semaphore_wait(sem, others + 2)

        @pl.when(jnp.logical_not(inside))
        def _():
            pl.semaphore_wait(sem, others + 1)

    tell(barrier)

    load_lat = pltpu.make_async_copy(lat_hbm, raw_in.at[pl.ds(1, rows), mine, :], local_sem.at[0])
    load_lat.start()
    held_vectors = (vector_0, vector_1, vector_2, vector_3, vector_4, vector_5)
    vectors = (gain_a, shift_a, gain_b, shift_b, bias_a, bias_b)
    load_vectors = [
        pltpu.make_async_copy(vector, held, local_sem.at[4 + index])
        for index, (vector, held) in enumerate(zip(vectors, held_vectors))
    ]
    for load in load_vectors:
        load.start()
    load_kernel = pltpu.make_async_copy(kw_hbm, kw, local_sem.at[1])
    load_rows = pltpu.make_async_copy(pj_hbm, pw.at[:, channel_rows(b), :], local_sem.at[2])
    load_output = pltpu.make_async_copy(ow_hbm, ow, local_sem.at[3])
    load_kernel.start()
    load_rows.start()
    load_output.start()

    count = rows * width * group_width
    both = 2 * groups_here
    sub16 = lax.broadcasted_iota(jnp.int32, (both, width), 0)
    lane16 = lax.broadcasted_iota(jnp.int32, (both, width), 1)
    sub8 = lax.broadcasted_iota(jnp.int32, (groups_here, width), 0)
    lane8 = lax.broadcasted_iota(jnp.int32, (groups_here, width), 1)

    def statistics(buffer, first):
        values = [
            buffer[first + row, mine, :].astype(jnp.float32).reshape(groups_here, group_width, width)
            for row in range(rows)
        ]
        total = sum(jnp.sum(value, axis=1) for value in values)
        mean = jnp.sum(total, axis=1, keepdims=True) / count
        mean = jnp.broadcast_to(mean, (groups_here, width))
        squares = 0.0
        for value in values:
            centered = value - mean[:, None, :]
            squares = squares + jnp.sum(centered * centered, axis=1)
        squares = jnp.broadcast_to(jnp.sum(squares, axis=1, keepdims=True), (groups_here, width))
        stacked = jnp.concatenate([mean, squares], axis=0)
        return jnp.sum(jnp.where(sub16 == lane16, stacked, 0.0), axis=0, keepdims=True)

    def combined(stat):
        found = []
        for shard in (h, sibling, cross, far):
            pieces = [stat[band * heads + shard] for band in range(bands)]
            total = sum(pieces)
            mean = total / bands
            offsets = sum((piece - mean) * (piece - mean) for piece in pieces)
            spread = pltpu.roll(jnp.broadcast_to(total, (8, width)), width - groups_here, 1)[:1]
            scale = lax.rsqrt((spread + offsets * count) / (count * bands) + 1e-05)
            pair_of = []
            for line in (mean, scale):
                wide = jnp.broadcast_to(line, (groups_here, width))
                column = jnp.sum(jnp.where(sub8 == lane8, wide, 0.0), axis=1, keepdims=True)
                pair_of.append(jnp.broadcast_to(column, (groups_here, width)))
            found.append(pair_of)
        return found

    def normalized(value, stats, which, span):
        mean, scale = stats
        grouped = value.astype(jnp.float32).reshape(groups_here, group_width, width)
        scaled = (grouped - mean[:, None, :]) * scale[:, None, :]
        return scaled.reshape(local, width) * spread_par[2 * which, span, :] + spread_par[
            2 * which + 1, span, :
        ]

    load_lat.wait()
    stat_a[b * heads + h] = statistics(raw_in, 1)
    for index, load in enumerate(load_vectors):
        load.wait()
        par[h, index] = held_vectors[index][...].reshape(1, local)

    told(barrier, len(close))

    def gather_pieces(buffer, pieces):
        sent = []
        for piece in pieces:
            own = buffer.at[piece, mine, :]
            there = buffer.at[piece, crossed, :]
            sent.append(
                (
                    remote(own, own, head=cross),
                    remote(own, own, head=sibling),
                    remote(there, there, head=sibling),
                )
            )
        return sent

    share = local // parts

    def share_rows(band, part):
        return pl.ds(pl.multiple_of(band * local + part * share, share), share)

    hops = []
    passed = []
    for kind in range(3):
        steps = []
        for hop in range(1, bands):
            two = []
            for sign, peer in ((1, below), (-1, above)):
                held = lax.rem(b - sign * (hop - 1) + bands, bands)
                got = lax.rem(b - sign * hop + bands, bands)
                if sign > 0:
                    sends = jnp.logical_and(b < bands - 1, b >= hop - 1)
                    receives = b >= hop
                else:
                    sends = jnp.logical_and(b > 0, b + hop - 1 < bands)
                    receives = b + hop < bands
                if hop == 1:
                    source = pj_hbm.at[kind, pl.ds(pl.multiple_of(g * share, share), share), :]
                else:
                    source = pw.at[kind, share_rows(held, g), :]
                move = remote(source, pw.at[kind, share_rows(held, g), :], band=peer)
                two.append((move, sends, receives, got))
            steps.append(two)
        hops.append(steps)
        passed.append([])

    def send_hop(kind, index):
        for move, sends, _, _ in hops[kind][index]:
            begin(move, sends)

    def take_hop(kind, index):
        for move, _, receives, _ in hops[kind][index]:
            arrive(move, receives)
        if index + 1 < len(hops[kind]):
            send_hop(kind, index + 1)
        for _, _, receives, got in hops[kind][index]:
            onward = pw.at[kind, share_rows(got, g), :]
            for peer in part_peers:
                move = remote(onward, onward, groups=peer)
                begin(move, receives)
                passed[kind].append((move, receives))

    plan = {'pre': '+K0', 'bs': '+V0', 'G': '-K0 +Q0', 'H1': '-V0 -K1', 'mid': '-Q0', 'T': '-K2 -V1', 'T2': '-Q1', 'R0': '-V2', 'R1': '-Q2'}

    def go(point):
        for word in plan.get(point, "").split():
            kind, index = "QKV".index(word[1]), int(word[2])
            if word[0] == "+":
                send_hop(kind, index)
            else:
                take_hop(kind, index)

    own_row = stat_a.at[b * heads + h]
    near_stats = [remote(own_row, own_row, head=peer) for peer in (cross, far, sibling)]
    near_par = [
        remote(par.at[h, pl.ds(0, 4)], par.at[h, pl.ds(0, 4)], head=peer)
        for peer in (cross, far, sibling)
    ]
    edges = (pl.ds(rows, 1), pl.ds(1, 1), pl.ds(2, rows - 2))
    gathered = gather_pieces(raw_in, edges)
    halo = []
    for source, target, peer, sends, receives in (
        (rows, 0, below, has_below, has_above),
        (1, rows + 1, above, has_above, has_below),
    ):
        for shard in (mine, crossed):
            move = remote(raw_in.at[source, shard, :], raw_in.at[target, shard, :], band=peer)
            onward = raw_in.at[target, shard, :]
            halo.append((move, remote(onward, onward, head=sibling), sends, receives))
    for copy in near_stats:
        begin(copy)
    for copy in near_par:
        begin(copy)
    tell(entry_sem.at[0])
    for to_cross, to_sibling, _ in gathered:
        begin(to_cross)
        begin(to_sibling)
    for index in (0, 2):
        move, _, sends, _ = halo[index]
        begin(move, sends)

    go('pre')
    told(entry_sem.at[0])
    tell(entry_sem.at[1])
    for copy in near_stats:
        arrive(copy)
    told(entry_sem.at[1])
    block = stat_a.at[pl.ds(b * heads, heads)]
    band_stats = [remote(block, block, band=peer) for peer in band_peers]
    for copy in band_stats:
        begin(copy)
    go('bs')

    for copy in near_par:
        arrive(copy)
    blocks = -(-local // width)
    lines = []
    for shard in range(heads):
        for index in range(4):
            lines.append(par[shard, index])
    lines += [par[h, 4], par[h, 5]]
    gap = jnp.zeros((1, blocks * width - local), jnp.float32)
    flat = []
    for line in lines:
        line = jnp.concatenate([line, gap], axis=1)
        flat += [line[:, k * width : (k + 1) * width] for k in range(blocks)]
    flat.append(jnp.zeros((-len(flat) % width, width), jnp.float32))
    columns = jnp.concatenate(flat, axis=0).T

    def column(index):
        pieces = [columns[:, index * blocks + k : index * blocks + k + 1] for k in range(blocks)]
        return jnp.broadcast_to(jnp.concatenate(pieces, axis=0)[:local], (local, width))

    for index in range(4):
        for shard in range(heads):
            spread_par[index, shard * local : (shard + 1) * local, :] = column(shard * 4 + index)
    for index in range(2):
        spread_par[4 + index, :local, :] = column(heads * 4 + index)

    for index in range(2):
        to_cross, _, onward = gathered[index]
        arrive(to_cross)
        begin(onward)
        move, _, sends, _ = halo[2 * index + 1]
        begin(move, sends)
    for index in (0, 2):
        move, onward, _, receives = halo[index]
        arrive(move, receives)
        begin(onward, receives)
    for target, receives in ((0, has_above), (rows + 1, has_below)):

        @pl.when(jnp.logical_not(receives))
        def _(target=target):
            grid_in[target] = jnp.zeros((channels, width), jnp.bfloat16)

    go('G')
    to_cross, _, onward = gathered[2]
    arrive(to_cross)
    begin(onward)
    for copy in band_stats:
        arrive(copy)
    first = combined(stat_a)

    def activate(row, slot, span):
        value = 0.5 * normalized(raw_in[row, span, :], first[slot], 0, span)
        grid_in[row, span, :] = (value + value * jnp.tanh(value)).astype(jnp.bfloat16)

    def activate_edge(target, receives, slots):
        @pl.when(receives)
        def _():
            for slot, span in slots:
                activate(target, slot, span)

    def half(which):
        return pl.ds(pl.multiple_of(which * pair, pair), pair)

    def convolve(which, overs, fresh, chosen=range(rows)):
        span = half(which)
        place = slice(chosen[0] * width, (chosen[-1] + 1) * width)
        total = None
        for over in overs:
            window = jnp.concatenate([grid_in[over + row, span, :] for row in chosen], axis=1)
            weights = kw[over, :, :, span].reshape(3 * local, pair)
            part = jnp.dot(weights, window, preferred_element_type=jnp.float32)
            total = part if total is None else total + part
        if not fresh:
            total = sums[:, place] + total
        sums[:, place] = total

    this_half, other_half = h // 2, cross // 2
    near_slots = ((0, mine), (1, sibs))
    far_slots = ((2, crossed), (3, fars))
    for _, to_sibling, _ in gathered:
        arrive(to_sibling)
    for row in range(rows):
        for slot, span in near_slots:
            activate(1 + row, slot, span)
    go('C')
    load_kernel.wait()
    convolve(this_half, (1,), True)
    for index in (0, 2):
        _, onward, _, receives = halo[index]
        arrive(onward, receives)
    activate_edge(0, has_above, near_slots)
    activate_edge(rows + 1, has_below, near_slots)
    for index in (1, 3):
        move, onward, _, receives = halo[index]
        arrive(move, receives)
        begin(onward, receives)
    convolve(this_half, (0, 2), False)
    go('H1')
    early = len(opened)
    for _, _, onward in gathered:
        arrive(onward)
    for row in range(rows):
        for slot, span in far_slots:
            activate(1 + row, slot, span)
    convolve(other_half, (1,), False)
    for index in (1, 3):
        _, onward, _, receives = halo[index]
        arrive(onward, receives)
    activate_edge(0, has_above, far_slots)
    activate_edge(rows + 1, has_below, far_slots)
    go('mid')
    place = lax.broadcasted_iota(jnp.int32, (local, width), 1)
    normed = gather_pieces(conv_in, tuple(pl.ds(row, 1) for row in range(rows)))

    def close_row(row):
        span = slice(row * width, (row + 1) * width)
        left = jnp.where(place == 0, 0.0, pltpu.roll(sums[:local, span], 1, 1))
        right = jnp.where(place == width - 1, 0.0, pltpu.roll(sums[2 * local :, span], width - 1, 1))
        value = (
            raw_in[1 + row, mine, :].astype(jnp.float32)
            + spread_par[4, :local, :]
            + (sums[local : 2 * local, span] + left + right)
        )
        conv_in[row, mine, :] = value.astype(jnp.bfloat16)
        wide_ref[row] = value.astype(jnp.bfloat16)

    def send_row(row):
        begin(normed[row][0])
        begin(normed[row][1])

    convolve(other_half, (0, 2), False, range(1))
    close_row(0)
    send_row(0)
    convolve(other_half, (0, 2), False, range(1, rows))
    for row in range(1, rows):
        close_row(row)
    stat_b[b * heads + h] = statistics(conv_in, 0)
    own_row = stat_b.at[b * heads + h]
    all_stats = [
        remote(own_row, own_row, band=lax.rem(b + up, bands), head=lax.rem(h + over, heads))
        for up in range(bands - 1, -1, -1)
        for over in range(heads - 1, -1, -1)
        if up or over
    ]
    for copy in all_stats:
        begin(copy)
    for row in range(1, rows):
        send_row(row)
    load_rows.wait()
    go('T')
    arrive(normed[0][0])
    begin(normed[0][2])
    go('T2')
    settle(early)
    for copy in all_stats:
        arrive(copy)
    second = combined(stat_b)
    arrive(normed[1][0])
    begin(normed[1][2])
    go('T3')
    for move, receives in passed[1]:
        arrive(move, receives)

    def normalize_row(row):
        arrive(normed[row][1])
        span = slice(row * width, (row + 1) * width)
        for slot, shard in ((0, mine), (1, sibs), (2, crossed)):
            feats[shard, span] = normalized(conv_in[row, shard, :], second[slot], 1, shard).astype(
                jnp.bfloat16
            )
        arrive(normed[row][2])
        feats[fars, span] = normalized(conv_in[row, fars, :], second[3], 1, fars).astype(jnp.bfloat16)

    def project(kind, span):
        return jnp.dot(turned[kind], feats[:, span], preferred_element_type=jnp.float32).astype(
            jnp.bfloat16
        )

    def place_heads(kind, made, chosen):
        for head in range(bands):
            for index, row in enumerate(chosen):
                qkv_out[kind, head, row] = made[
                    head * HEAD_SIZE : (head + 1) * HEAD_SIZE, index * width : (index + 1) * width
                ]

    def spread_rows(kind, row, size):
        chosen = pl.ds(row, size)
        qkv_in[kind, b, chosen] = qkv_out[kind, b, chosen]
        moves = [
            remote(qkv_out.at[kind, peer, chosen], qkv_in.at[kind, b, chosen], band=peer)
            for peer in band_peers
        ]
        for copy in moves:
            begin(copy)
        return moves

    turned[1] = pw[1].T
    moved_keys = []
    early = len(opened)
    for row in range(rows):
        normalize_row(row)
        if row + 2 < rows:
            arrive(normed[row + 2][0])
            begin(normed[row + 2][2])
        place_heads(1, project(1, slice(row * width, (row + 1) * width)), (row,))
        moved_keys += spread_rows(1, row, 1)
        go('R%d' % row)
    go('RE')
    everything = slice(0, tokens)
    for move, receives in passed[2]:
        arrive(move, receives)
    turned[2] = pw[2].T
    place_heads(2, project(2, everything), range(rows))
    moved_values = spread_rows(2, 0, rows)
    for move, receives in passed[0]:
        arrive(move, receives)
    turned[0] = pw[0].T
    place_heads(0, project(0, everything), range(rows))
    moved_queries = [spread_rows(0, row, 1) for row in range(rows)]

    inner = bands * HEAD_SIZE
    factor = HEAD_SIZE ** (-0.5) * math.log2(math.e)

    def feature_rows(shard):
        return pl.ds(pl.multiple_of(shard * inner, inner), inner)

    own_features = pl.ds(pl.multiple_of(h * inner + b * HEAD_SIZE, HEAD_SIZE), HEAD_SIZE)
    final_row = rows - 1
    returned = [
        [
            remote(att_out.at[row, index], att_in.at[row, own_features, :], band=peer)
            for index, peer in enumerate(band_peers)
        ]
        for row in range(rows)
    ]
    direct = [
        remote(
            att_out.at[final_row, index],
            att_in.at[final_row, own_features, :],
            band=peer,
            head=cross,
        )
        for index, peer in enumerate(band_peers)
    ]
    own_final = att_in.at[final_row, own_features, :]
    direct.append(remote(own_final, own_final, head=cross))
    final = []
    for row in range(rows):
        own = att_in.at[row, feature_rows(h), :]
        there = att_in.at[row, feature_rows(cross), :]
        to_cross = remote(own, own, head=cross) if row < final_row else None
        final.append(
            (to_cross, remote(own, own, head=sibling), remote(there, there, head=sibling))
        )

    def pass_on(row):
        for copy in returned[row]:
            arrive(copy)
        if row < final_row:
            begin(final[row][0])
        begin(final[row][1])

    def relay(row):
        for copy in direct if row == final_row else final[row][:1]:
            arrive(copy)
        begin(final[row][2])

    def finish(row):
        arrive(final[row][1])
        arrive(final[row][2])
        outgoing = jnp.dot(ow[...], att_in[row], preferred_element_type=jnp.float32)
        gain_ref[row] = (
            conv_in[row, mine, :].astype(jnp.float32) + spread_par[5, :local, :] + outgoing
        ).astype(jnp.bfloat16)

    settle(early)
    for copy in moved_keys:
        arrive(copy)
    keys = jnp.concatenate(
        [qkv_in[1, source, row] for source in range(bands) for row in range(rows)], axis=1
    ).T
    for copy in moved_values:
        arrive(copy)
    values = jnp.concatenate(
        [qkv_in[2, source, row] for source in range(bands) for row in range(rows)], axis=1
    )

    def attend(pieces):
        query = jnp.concatenate(pieces, axis=1)
        scores = jnp.dot(keys, query, preferred_element_type=jnp.float32)
        top = jnp.max(scores, axis=0, keepdims=True)
        heavy = jnp.exp2((scores - top) * factor)
        total = jnp.sum(heavy, axis=0, keepdims=True)
        mixed = jnp.dot(values, heavy.astype(jnp.bfloat16), preferred_element_type=jnp.float32)
        result = (mixed / total).astype(jnp.bfloat16)
        return [result[:, k * width : (k + 1) * width] for k in range(len(pieces))]

    for row, result in enumerate(attend([qkv_out[0, b, row] for row in range(rows)])):
        att_in[row, own_features, :] = result
    settle(len(opened) - rows * len(band_peers))
    queries_end = len(opened)
    begin(direct[-1])
    for row in range(rows):
        for copy in moved_queries[row]:
            arrive(copy)
        for index, result in enumerate(attend([qkv_in[0, peer, row] for peer in band_peers])):
            att_out[row, index] = result
        for copy in returned[row]:
            begin(copy)
        if row == final_row:
            for copy in direct[:-1]:
                begin(copy)
        if row >= 1:
            pass_on(row - 1)
        if row == final_row:
            settle(queries_end)
    load_output.wait()
    relay(0)
    pass_on(final_row)
    for row in range(1, rows):
        relay(row)
    for row in range(rows):
        finish(row)

    settle(len(opened))


def pair_shards(
    parts,
    bands,
    heads,
    latent,
    first_gain,
    first_shift,
    kernel,
    kernel_bias,
    second_gain,
    second_shift,
    projection,
    output_weight,
    output_bias,
):
    rows, width, local = latent.shape
    channels, tokens = local * heads, rows * width
    inner = projection.shape[2]
    vectors = [first_gain, first_shift, second_gain, second_shift, kernel_bias, output_bias]
    vmem = pl.BlockSpec(memory_space=pltpu.VMEM)
    hbm = pl.BlockSpec(memory_space=pl.ANY)
    result = jax.ShapeDtypeStruct((rows, local, width), jnp.bfloat16)
    copies = 160
    call = pl.pallas_call(
        functools.partial(pair_kernel, (parts, bands, heads, rows, local, width)),
        out_shape=(result, result),
        in_specs=[hbm] * 10,
        out_specs=(vmem, vmem),
        scratch_shapes=[
            pltpu.VMEM((3, 3, local, channels), jnp.bfloat16),
            pltpu.VMEM((3, channels, inner), jnp.bfloat16),
            pltpu.VMEM((3, inner, channels), jnp.bfloat16),
            pltpu.VMEM((local, inner * heads), jnp.bfloat16),
            pltpu.VMEM((heads, 6, 1, local), jnp.float32),
            pltpu.VMEM((6, channels, width), jnp.float32),
            pltpu.VMEM((bands * heads, 1, width), jnp.float32),
            pltpu.VMEM((bands * heads, 1, width), jnp.float32),
            pltpu.VMEM((rows + 2, channels, width), jnp.bfloat16),
            pltpu.VMEM((rows + 2, channels, width), jnp.bfloat16),
            pltpu.VMEM((3 * local, tokens), jnp.float32),
            pltpu.VMEM((rows, channels, width), jnp.bfloat16),
            pltpu.VMEM((channels, tokens), jnp.bfloat16),
            pltpu.VMEM((3, bands, rows, HEAD_SIZE, width), jnp.bfloat16),
            pltpu.VMEM((3, bands, rows, HEAD_SIZE, width), jnp.bfloat16),
            pltpu.VMEM((rows, bands - 1, HEAD_SIZE, width), jnp.bfloat16),
            pltpu.VMEM((rows, inner * heads, width), jnp.bfloat16),
        ]
        + [pltpu.VMEM((local,), jnp.float32)] * 6
        + [
            pltpu.SemaphoreType.DMA((10,)),
            pltpu.SemaphoreType.REGULAR((2,)),
            pltpu.SemaphoreType.DMA((copies,)),
            pltpu.SemaphoreType.DMA((copies,)),
        ],
        compiler_params=pltpu.CompilerParams(
            collective_id=0, has_side_effects=True, vmem_limit_bytes=60 << 20
        ),
    )
    wide, gained = call(
        jnp.transpose(latent, (0, 2, 1)),
        *vectors,
        jnp.transpose(kernel, (1, 2, 0, 3)),
        jnp.transpose(projection, (1, 0, 2)),
        output_weight,
    )
    top = jnp.finfo(jnp.bfloat16).max
    return tuple(jnp.minimum(jnp.transpose(made, (0, 2, 1)), top) for made in (wide, gained))


def solution(mesh):
    placed = (
        P(("groups", "band"), None, "head"),
        P("head"),
        P("head"),
        P("head", None, None, None),
        P("head"),
        P("head"),
        P("head"),
        P("band", None, "head"),
        P("head", None),
        P("head"),
    )
    parts, bands, heads = (mesh.shape[axis] for axis in ("groups", "band", "head"))
    paired = heads == 4 and bands > 1 and HEADS == heads * bands and CHANNELS % (16 * parts * heads) == 0
    body = functools.partial(pair_shards, parts, bands, heads) if paired else shards
    return jax.shard_map(
        body,
        mesh=mesh,
        in_specs=placed,
        out_specs=(P(("groups", "band"), None, "head"), P(("groups", "band"), None, "head")),
        check_vma=False,
    )
```

```python
import functools
import math

import jax
import jax.numpy as jnp
from jax import lax
from jax.experimental import pallas as pl
from jax.experimental.pallas import tpu as pltpu
from jax.sharding import PartitionSpec as P

CHANNELS = 1280
HEADS = 16
HEAD_SIZE = 64
NORM_GROUPS = 32


def padded_2(cells, sides, width):
    for axis, dim in sides:
        count = lax.axis_size(axis)
        ends = count - 1
        head = lax.slice_in_dim(cells, 0, width, axis=dim)
        tail = lax.slice_in_dim(cells, cells.shape[dim] - width, cells.shape[dim], axis=dim)
        cells = jnp.concatenate(
            [
                lax.ppermute(tail, axis, [(i, (i + 1) % count) for i in range(ends)]),
                cells,
                lax.ppermute(head, axis, [((i + 1) % count, i) for i in range(ends)]),
            ],
            axis=dim,
        )
    return cells


def normalize(values, gain, shift, group_width, count):
    band_rows, width, channels = values.shape
    grouped = values.reshape(band_rows * width, channels // group_width, group_width)
    mean = lax.psum(jnp.sum(grouped, axis=(0, 2)), "band") / count
    centered = grouped - mean[None, :, None]
    spread = lax.psum(jnp.sum(centered * centered, axis=(0, 2)), "band") / count
    scaled = centered * lax.rsqrt(spread + 1e-05)[None, :, None]
    return scaled.reshape(band_rows, width, channels) * gain + shift


def contract_last(left, right):
    return lax.dot_general(
        left, right, (((1,), (1,)), ((), ())), preferred_element_type=jnp.float32
    )


def kernel_block(padded, weights, band_rows, width):
    inputs = padded.shape[2]
    wide = jnp.pad(padded, ((0, 0), (1, 1), (0, 0)))
    summed = jnp.zeros((band_rows * width, weights.shape[0]), jnp.float32)
    for above in range(3):
        for beside in range(3):
            window = wide[above : above + band_rows, beside : beside + width, :].reshape(
                band_rows * width, inputs
            )
            summed = summed + contract_last(window, weights[:, above, beside, :])
    return summed


def shards(
    latent,
    first_gain,
    first_shift,
    kernel,
    kernel_bias,
    second_gain,
    second_shift,
    projection,
    output_weight,
    output_bias,
):
    band_rows, width, channels = latent.shape
    tokens = band_rows * width
    group_width = CHANNELS // NORM_GROUPS
    count = lax.axis_size("band") * band_rows * width * group_width
    outputs = kernel.shape[0]
    latent_wide = latent.astype(jnp.float32)
    activated = jax.nn.silu(
        normalize(latent_wide, first_gain, first_shift, group_width, count)
    ).astype(jnp.bfloat16)
    gathered = lax.all_gather(activated, "head", axis=2, tiled=True)
    padded = padded_2(gathered, (("band", 0),), 1)
    summed = kernel_block(padded, kernel, band_rows, width)
    convolved = (latent_wide + kernel_bias + summed.reshape(band_rows, width, outputs)).astype(
        jnp.bfloat16
    )
    normed = normalize(
        convolved.astype(jnp.float32), second_gain, second_shift, group_width, count
    ).astype(jnp.bfloat16)
    features = lax.all_gather(normed, "head", axis=2, tiled=True).reshape(tokens, CHANNELS)
    local_inner = projection.shape[2]
    local_heads = local_inner // HEAD_SIZE
    piece = lax.all_gather(projection, "band", axis=0, tiled=True)
    projected = jnp.dot(
        features, piece.reshape(piece.shape[0], 3 * local_inner), preferred_element_type=jnp.float32
    )
    projected = projected.astype(jnp.bfloat16).reshape(tokens, 3, local_inner)
    query = projected[:, 0].reshape(tokens, local_heads, HEAD_SIZE)
    key_value = projected[:, 1:]
    factor = HEAD_SIZE ** (-0.5)
    piece = lax.all_gather(key_value, "band", axis=0, tiled=True)
    running = jnp.full((local_heads, tokens), -1e30, jnp.float32)
    keys = piece[:, 0].reshape(piece.shape[0], local_heads, HEAD_SIZE)
    values = piece[:, 1].reshape(piece.shape[0], local_heads, HEAD_SIZE)
    scores = jnp.einsum("qhd,khd->hqk", query, keys, preferred_element_type=jnp.float32) * factor
    highest = jnp.maximum(running, jnp.max(scores, axis=2))
    weights = jnp.exp(scores - highest[:, :, None])
    total = jnp.sum(weights, axis=2)
    summed_values = jnp.einsum(
        "hqk,khd->hqd", weights.astype(jnp.bfloat16), values, preferred_element_type=jnp.float32
    )
    running, total, summed_values = (highest, total, summed_values)
    attention = (
        jnp.transpose(summed_values / total[:, :, None], (1, 0, 2))
        .reshape(tokens, local_inner)
        .astype(jnp.bfloat16)
    )
    outgoing = contract_last(lax.all_gather(attention, "head", axis=1, tiled=True), output_weight)
    attended = (
        convolved.astype(jnp.float32) + output_bias + outgoing.reshape(band_rows, width, outputs)
    )
    return (convolved, attended.astype(jnp.bfloat16))


def pair_kernel(
    shape,
    lat_hbm,
    gain_a,
    shift_a,
    gain_b,
    shift_b,
    bias_a,
    bias_b,
    kw_hbm,
    pj_hbm,
    ow_hbm,
    wide_ref,
    gain_ref,
    kw,
    pw,
    turned,
    ow,
    par,
    spread_par,
    stat_a,
    stat_b,
    raw_in,
    grid_in,
    sums,
    conv_in,
    feats,
    qkv_out,
    qkv_in,
    att_out,
    att_in,
    vector_0,
    vector_1,
    vector_2,
    vector_3,
    vector_4,
    vector_5,
    local_sem,
    entry_sem,
    send_sem,
    recv_sem,
):
    parts, bands, heads, rows, local, width = shape
    channels = local * heads
    tokens = rows * width
    group_width = CHANNELS // NORM_GROUPS
    groups_here = local // group_width
    pair = 2 * local
    g, b, h = lax.axis_index("groups"), lax.axis_index("band"), lax.axis_index("head")
    sibling = h + 1 - 2 * lax.rem(h, 2)
    cross = lax.rem(h + 2, heads)
    far = lax.rem(sibling + 2, heads)
    has_above, has_below = b > 0, b < bands - 1
    above, below = lax.rem(b + bands - 1, bands), lax.rem(b + 1, bands)
    mesh_id = pl.DeviceIdType.MESH
    used = [0]

    def remote(src, dst, groups=None, band=None, head=None):
        index = used[0]
        used[0] += 1
        return pltpu.make_async_remote_copy(
            src_ref=src,
            dst_ref=dst,
            send_sem=send_sem.at[index],
            recv_sem=recv_sem.at[index],
            device_id=(
                g if groups is None else groups,
                b if band is None else band,
                h if head is None else head,
            ),
            device_id_type=mesh_id,
        )

    opened = []

    def begin(copy, sends=None):
        opened.append((copy, sends))
        if sends is None:
            copy.start()
        else:

            @pl.when(sends)
            def _():
                copy.start()

    settled = [0]

    def settle(until):
        for copy, sends in opened[settled[0] : until]:
            if sends is None:
                copy.wait_send()
            else:

                @pl.when(sends)
                def _(copy=copy):
                    copy.wait_send()

        settled[0] = max(settled[0], until)

    def arrive(copy, receives=None):
        if receives is None:
            copy.wait_recv()
        else:

            @pl.when(receives)
            def _():
                copy.wait_recv()

    def channel_rows(shard):
        return pl.ds(pl.multiple_of(shard * local, local), local)

    band_peers = [lax.rem(b + 2, bands), bands - 1 - b, b + 1 - 2 * lax.rem(b, 2)]
    part_peers = [lax.rem(g + step, parts) for step in range(1, parts)]
    mine, crossed, sibs, fars = (channel_rows(s) for s in (h, cross, sibling, far))

    barrier = pltpu.get_barrier_semaphore()
    close = [(g, b, sibling), (g, b, cross), (g, b, far)] + [(peer, b, h) for peer in part_peers]
    for neighbour in close:
        pl.semaphore_signal(barrier, inc=1, device_id=neighbour, device_id_type=mesh_id)

    def tell(sem):
        @pl.when(has_above)
        def _():
            pl.semaphore_signal(sem, inc=1, device_id=(g, above, h), device_id_type=mesh_id)

        @pl.when(has_below)
        def _():
            pl.semaphore_signal(sem, inc=1, device_id=(g, below, h), device_id_type=mesh_id)

    def told(sem, others=0):
        inside = jnp.logical_and(has_above, has_below)

        @pl.when(inside)
        def _():
            pl.semaphore_wait(sem, others + 2)

        @pl.when(jnp.logical_not(inside))
        def _():
            pl.semaphore_wait(sem, others + 1)

    tell(barrier)

    load_lat = pltpu.make_async_copy(lat_hbm, raw_in.at[pl.ds(1, rows), mine, :], local_sem.at[0])
    load_lat.start()
    held_vectors = (vector_0, vector_1, vector_2, vector_3, vector_4, vector_5)
    vectors = (gain_a, shift_a, gain_b, shift_b, bias_a, bias_b)
    load_vectors = [
        pltpu.make_async_copy(vector, held, local_sem.at[4 + index])
        for index, (vector, held) in enumerate(zip(vectors, held_vectors))
    ]
    for load in load_vectors:
        load.start()
    load_kernel = pltpu.make_async_copy(kw_hbm, kw, local_sem.at[1])
    load_rows = pltpu.make_async_copy(pj_hbm, pw.at[:, channel_rows(b), :], local_sem.at[2])
    load_output = pltpu.make_async_copy(ow_hbm, ow, local_sem.at[3])
    load_kernel.start()
    load_rows.start()
    load_output.start()

    count = rows * width * group_width
    both = 2 * groups_here
    sub16 = lax.broadcasted_iota(jnp.int32, (both, width), 0)
    lane16 = lax.broadcasted_iota(jnp.int32, (both, width), 1)
    sub8 = lax.broadcasted_iota(jnp.int32, (groups_here, width), 0)
    lane8 = lax.broadcasted_iota(jnp.int32, (groups_here, width), 1)

    def statistics(buffer, first):
        values = [
            buffer[first + row, mine, :].astype(jnp.float32).reshape(groups_here, group_width, width)
            for row in range(rows)
        ]
        total = sum(jnp.sum(value, axis=1) for value in values)
        mean = jnp.sum(total, axis=1, keepdims=True) / count
        mean = jnp.broadcast_to(mean, (groups_here, width))
        squares = 0.0
        for value in values:
            centered = value - mean[:, None, :]
            squares = squares + jnp.sum(centered * centered, axis=1)
        squares = jnp.broadcast_to(jnp.sum(squares, axis=1, keepdims=True), (groups_here, width))
        stacked = jnp.concatenate([mean, squares], axis=0)
        return jnp.sum(jnp.where(sub16 == lane16, stacked, 0.0), axis=0, keepdims=True)

    def combined(stat):
        found = []
        for shard in (h, sibling, cross, far):
            pieces = [stat[band * heads + shard] for band in range(bands)]
            total = sum(pieces)
            mean = total / bands
            offsets = sum((piece - mean) * (piece - mean) for piece in pieces)
            spread = pltpu.roll(jnp.broadcast_to(total, (8, width)), width - groups_here, 1)[:1]
            scale = lax.rsqrt((spread + offsets * count) / (count * bands) + 1e-05)
            pair_of = []
            for line in (mean, scale):
                wide = jnp.broadcast_to(line, (groups_here, width))
                column = jnp.sum(jnp.where(sub8 == lane8, wide, 0.0), axis=1, keepdims=True)
                pair_of.append(jnp.broadcast_to(column, (groups_here, width)))
            found.append(pair_of)
        return found

    def normalized(value, stats, which, span):
        mean, scale = stats
        grouped = value.astype(jnp.float32).reshape(groups_here, group_width, width)
        scaled = (grouped - mean[:, None, :]) * scale[:, None, :]
        return scaled.reshape(local, width) * spread_par[2 * which, span, :] + spread_par[
            2 * which + 1, span, :
        ]

    load_lat.wait()
    stat_a[b * heads + h] = statistics(raw_in, 1)
    for index, load in enumerate(load_vectors):
        load.wait()
        par[h, index] = held_vectors[index][...].reshape(1, local)

    told(barrier, len(close))

    def gather_pieces(buffer, pieces):
        sent = []
        for piece in pieces:
            own = buffer.at[piece, mine, :]
            there = buffer.at[piece, crossed, :]
            sent.append(
                (
                    remote(own, own, head=cross),
                    remote(own, own, head=sibling),
                    remote(there, there, head=sibling),
                )
            )
        return sent

    share = local // parts

    def share_rows(band, part):
        return pl.ds(pl.multiple_of(band * local + part * share, share), share)

    hops = []
    passed = []
    for kind in range(3):
        steps = []
        for hop in range(1, bands):
            two = []
            for sign, peer in ((1, below), (-1, above)):
                held = lax.rem(b - sign * (hop - 1) + bands, bands)
                got = lax.rem(b - sign * hop + bands, bands)
                if sign > 0:
                    sends = jnp.logical_and(b < bands - 1, b >= hop - 1)
                    receives = b >= hop
                else:
                    sends = jnp.logical_and(b > 0, b + hop - 1 < bands)
                    receives = b + hop < bands
                if hop == 1:
                    source = pj_hbm.at[kind, pl.ds(pl.multiple_of(g * share, share), share), :]
                else:
                    source = pw.at[kind, share_rows(held, g), :]
                move = remote(source, pw.at[kind, share_rows(held, g), :], band=peer)
                two.append((move, sends, receives, got))
            steps.append(two)
        hops.append(steps)
        passed.append([])

    def send_hop(kind, index):
        for move, sends, _, _ in hops[kind][index]:
            begin(move, sends)

    def take_hop(kind, index):
        for move, _, receives, _ in hops[kind][index]:
            arrive(move, receives)
        if index + 1 < len(hops[kind]):
            send_hop(kind, index + 1)
        for _, _, receives, got in hops[kind][index]:
            onward = pw.at[kind, share_rows(got, g), :]
            for peer in part_peers:
                move = remote(onward, onward, groups=peer)
                begin(move, receives)
                passed[kind].append((move, receives))

    plan = {'pre': '+K0', 'bs': '+V0', 'G': '-K0 +Q0', 'H1': '-V0 -K1', 'mid': '-Q0', 'T': '-K2 -V1', 'T2': '-Q1', 'R0': '-V2', 'R1': '-Q2'}

    def go(point):
        for word in plan.get(point, "").split():
            kind, index = "QKV".index(word[1]), int(word[2])
            if word[0] == "+":
                send_hop(kind, index)
            else:
                take_hop(kind, index)

    own_row = stat_a.at[b * heads + h]
    near_stats = [remote(own_row, own_row, head=peer) for peer in (cross, far, sibling)]
    near_par = [
        remote(par.at[h, pl.ds(0, 4)], par.at[h, pl.ds(0, 4)], head=peer)
        for peer in (cross, far, sibling)
    ]
    edges = (pl.ds(rows, 1), pl.ds(1, 1), pl.ds(2, rows - 2))
    gathered = gather_pieces(raw_in, edges)
    halo = []
    for source, target, peer, sends, receives in (
        (rows, 0, below, has_below, has_above),
        (1, rows + 1, above, has_above, has_below),
    ):
        for shard in (mine, crossed):
            move = remote(raw_in.at[source, shard, :], raw_in.at[target, shard, :], band=peer)
            onward = raw_in.at[target, shard, :]
            halo.append((move, remote(onward, onward, head=sibling), sends, receives))
    for copy in near_stats:
        begin(copy)
    for copy in near_par:
        begin(copy)
    tell(entry_sem.at[0])
    for to_cross, to_sibling, _ in gathered:
        begin(to_cross)
        begin(to_sibling)
    for index in (0, 2):
        move, _, sends, _ = halo[index]
        begin(move, sends)

    go('pre')
    told(entry_sem.at[0])
    tell(entry_sem.at[1])
    for copy in near_stats:
        arrive(copy)
    told(entry_sem.at[1])
    block = stat_a.at[pl.ds(b * heads, heads)]
    band_stats = [remote(block, block, band=peer) for peer in band_peers]
    for copy in band_stats:
        begin(copy)
    go('bs')

    for copy in near_par:
        arrive(copy)
    blocks = -(-local // width)
    lines = []
    for shard in range(heads):
        for index in range(4):
            lines.append(par[shard, index])
    lines += [par[h, 4], par[h, 5]]
    gap = jnp.zeros((1, blocks * width - local), jnp.float32)
    flat = []
    for line in lines:
        line = jnp.concatenate([line, gap], axis=1)
        flat += [line[:, k * width : (k + 1) * width] for k in range(blocks)]
    flat.append(jnp.zeros((-len(flat) % width, width), jnp.float32))
    columns = jnp.concatenate(flat, axis=0).T

    def column(index):
        pieces = [columns[:, index * blocks + k : index * blocks + k + 1] for k in range(blocks)]
        return jnp.broadcast_to(jnp.concatenate(pieces, axis=0)[:local], (local, width))

    for index in range(4):
        for shard in range(heads):
            spread_par[index, shard * local : (shard + 1) * local, :] = column(shard * 4 + index)
    for index in range(2):
        spread_par[4 + index, :local, :] = column(heads * 4 + index)

    for index in range(2):
        to_cross, _, onward = gathered[index]
        arrive(to_cross)
        begin(onward)
        move, _, sends, _ = halo[2 * index + 1]
        begin(move, sends)
    for index in (0, 2):
        move, onward, _, receives = halo[index]
        arrive(move, receives)
        begin(onward, receives)
    for target, receives in ((0, has_above), (rows + 1, has_below)):

        @pl.when(jnp.logical_not(receives))
        def _(target=target):
            grid_in[target] = jnp.zeros((channels, width), jnp.bfloat16)

    go('G')
    to_cross, _, onward = gathered[2]
    arrive(to_cross)
    begin(onward)
    for copy in band_stats:
        arrive(copy)
    first = combined(stat_a)

    def activate(row, slot, span):
        value = 0.5 * normalized(raw_in[row, span, :], first[slot], 0, span)
        grid_in[row, span, :] = (value + value * jnp.tanh(value)).astype(jnp.bfloat16)

    def activate_edge(target, receives, slots):
        @pl.when(receives)
        def _():
            for slot, span in slots:
                activate(target, slot, span)

    def half(which):
        return pl.ds(pl.multiple_of(which * pair, pair), pair)

    def convolve(which, overs, fresh, chosen=range(rows)):
        span = half(which)
        place = slice(chosen[0] * width, (chosen[-1] + 1) * width)
        total = None
        for over in overs:
            window = jnp.concatenate([grid_in[over + row, span, :] for row in chosen], axis=1)
            weights = kw[over, :, :, span].reshape(3 * local, pair)
            part = jnp.dot(weights, window, preferred_element_type=jnp.float32)
            total = part if total is None else total + part
        if not fresh:
            total = sums[:, place] + total
        sums[:, place] = total

    this_half, other_half = h // 2, cross // 2
    near_slots = ((0, mine), (1, sibs))
    far_slots = ((2, crossed), (3, fars))
    for _, to_sibling, _ in gathered:
        arrive(to_sibling)
    for row in range(rows):
        for slot, span in near_slots:
            activate(1 + row, slot, span)
    go('C')
    load_kernel.wait()
    convolve(this_half, (1,), True)
    for index in (0, 2):
        _, onward, _, receives = halo[index]
        arrive(onward, receives)
    activate_edge(0, has_above, near_slots)
    activate_edge(rows + 1, has_below, near_slots)
    convolve(this_half, (0, 2), False)
    for index in (1, 3):
        move, onward, _, receives = halo[index]
        arrive(move, receives)
        begin(onward, receives)
    for _, _, onward in gathered:
        arrive(onward)
    for row in range(rows):
        for slot, span in far_slots:
            activate(1 + row, slot, span)
    go('H1')
    early = len(opened)
    convolve(other_half, (1,), False)
    for index in (1, 3):
        _, onward, _, receives = halo[index]
        arrive(onward, receives)
    activate_edge(0, has_above, far_slots)
    activate_edge(rows + 1, has_below, far_slots)
    go('mid')
    place = lax.broadcasted_iota(jnp.int32, (local, width), 1)
    normed = gather_pieces(conv_in, tuple(pl.ds(row, 1) for row in range(rows)))

    def close_row(row):
        span = slice(row * width, (row + 1) * width)
        left = jnp.where(place == 0, 0.0, pltpu.roll(sums[:local, span], 1, 1))
        right = jnp.where(place == width - 1, 0.0, pltpu.roll(sums[2 * local :, span], width - 1, 1))
        value = (
            raw_in[1 + row, mine, :].astype(jnp.float32)
            + spread_par[4, :local, :]
            + (sums[local : 2 * local, span] + left + right)
        )
        conv_in[row, mine, :] = value.astype(jnp.bfloat16)
        wide_ref[row] = value.astype(jnp.bfloat16)

    def send_row(row):
        begin(normed[row][0])
        begin(normed[row][1])

    convolve(other_half, (0, 2), False, range(1))
    close_row(0)
    send_row(0)
    convolve(other_half, (0, 2), False, range(1, rows))
    for row in range(1, rows):
        close_row(row)
    stat_b[b * heads + h] = statistics(conv_in, 0)
    own_row = stat_b.at[b * heads + h]
    all_stats = [
        remote(own_row, own_row, band=lax.rem(b + up, bands), head=lax.rem(h + over, heads))
        for up in range(bands - 1, -1, -1)
        for over in range(heads - 1, -1, -1)
        if up or over
    ]
    for copy in all_stats:
        begin(copy)
    for row in range(1, rows):
        send_row(row)
    load_rows.wait()
    go('T')
    arrive(normed[0][0])
    begin(normed[0][2])
    go('T2')
    settle(early)
    for copy in all_stats:
        arrive(copy)
    second = combined(stat_b)
    arrive(normed[1][0])
    begin(normed[1][2])
    go('T3')
    for move, receives in passed[1]:
        arrive(move, receives)

    def normalize_row(row):
        arrive(normed[row][1])
        span = slice(row * width, (row + 1) * width)
        for slot, shard in ((0, mine), (1, sibs), (2, crossed)):
            feats[shard, span] = normalized(conv_in[row, shard, :], second[slot], 1, shard).astype(
                jnp.bfloat16
            )
        arrive(normed[row][2])
        feats[fars, span] = normalized(conv_in[row, fars, :], second[3], 1, fars).astype(jnp.bfloat16)

    def project(kind, span):
        return jnp.dot(turned[kind], feats[:, span], preferred_element_type=jnp.float32).astype(
            jnp.bfloat16
        )

    def place_heads(kind, made, chosen):
        for head in range(bands):
            for index, row in enumerate(chosen):
                qkv_out[kind, head, row] = made[
                    head * HEAD_SIZE : (head + 1) * HEAD_SIZE, index * width : (index + 1) * width
                ]

    def spread_rows(kind, row, size):
        chosen = pl.ds(row, size)
        qkv_in[kind, b, chosen] = qkv_out[kind, b, chosen]
        moves = [
            remote(qkv_out.at[kind, peer, chosen], qkv_in.at[kind, b, chosen], band=peer)
            for peer in band_peers
        ]
        for copy in moves:
            begin(copy)
        return moves

    turned[1] = pw[1].T
    moved_keys = []
    early = len(opened)
    for row in range(rows):
        normalize_row(row)
        if row + 2 < rows:
            arrive(normed[row + 2][0])
            begin(normed[row + 2][2])
        place_heads(1, project(1, slice(row * width, (row + 1) * width)), (row,))
        moved_keys += spread_rows(1, row, 1)
        go('R%d' % row)
    go('RE')
    everything = slice(0, tokens)
    for move, receives in passed[2]:
        arrive(move, receives)
    turned[2] = pw[2].T
    place_heads(2, project(2, everything), range(rows))
    moved_values = spread_rows(2, 0, rows)
    for move, receives in passed[0]:
        arrive(move, receives)
    turned[0] = pw[0].T
    place_heads(0, project(0, everything), range(rows))
    moved_queries = [spread_rows(0, row, 1) for row in range(rows)]

    inner = bands * HEAD_SIZE
    factor = HEAD_SIZE ** (-0.5) * math.log2(math.e)

    def feature_rows(shard):
        return pl.ds(pl.multiple_of(shard * inner, inner), inner)

    own_features = pl.ds(pl.multiple_of(h * inner + b * HEAD_SIZE, HEAD_SIZE), HEAD_SIZE)
    final_row = rows - 1
    returned = [
        [
            remote(att_out.at[row, index], att_in.at[row, own_features, :], band=peer)
            for index, peer in enumerate(band_peers)
        ]
        for row in range(rows)
    ]
    direct = [
        remote(
            att_out.at[final_row, index],
            att_in.at[final_row, own_features, :],
            band=peer,
            head=cross,
        )
        for index, peer in enumerate(band_peers)
    ]
    own_final = att_in.at[final_row, own_features, :]
    direct.append(remote(own_final, own_final, head=cross))
    final = []
    for row in range(rows):
        own = att_in.at[row, feature_rows(h), :]
        there = att_in.at[row, feature_rows(cross), :]
        to_cross = remote(own, own, head=cross) if row < final_row else None
        final.append(
            (to_cross, remote(own, own, head=sibling), remote(there, there, head=sibling))
        )

    def pass_on(row):
        for copy in returned[row]:
            arrive(copy)
        if row < final_row:
            begin(final[row][0])
        begin(final[row][1])

    def relay(row):
        for copy in direct if row == final_row else final[row][:1]:
            arrive(copy)
        begin(final[row][2])

    def finish(row):
        arrive(final[row][1])
        arrive(final[row][2])
        outgoing = jnp.dot(ow[...], att_in[row], preferred_element_type=jnp.float32)
        gain_ref[row] = (
            conv_in[row, mine, :].astype(jnp.float32) + spread_par[5, :local, :] + outgoing
        ).astype(jnp.bfloat16)

    settle(early)
    for copy in moved_keys:
        arrive(copy)
    keys = jnp.concatenate(
        [qkv_in[1, source, row] for source in range(bands) for row in range(rows)], axis=1
    ).T
    for copy in moved_values:
        arrive(copy)
    values = jnp.concatenate(
        [qkv_in[2, source, row] for source in range(bands) for row in range(rows)], axis=1
    )

    def attend(pieces):
        query = jnp.concatenate(pieces, axis=1)
        scores = jnp.dot(keys, query, preferred_element_type=jnp.float32)
        top = jnp.max(scores, axis=0, keepdims=True)
        heavy = jnp.exp2((scores - top) * factor)
        total = jnp.sum(heavy, axis=0, keepdims=True)
        mixed = jnp.dot(values, heavy.astype(jnp.bfloat16), preferred_element_type=jnp.float32)
        result = (mixed / total).astype(jnp.bfloat16)
        return [result[:, k * width : (k + 1) * width] for k in range(len(pieces))]

    for row, result in enumerate(attend([qkv_out[0, b, row] for row in range(rows)])):
        att_in[row, own_features, :] = result
    settle(len(opened) - rows * len(band_peers))
    queries_end = len(opened)
    begin(direct[-1])
    for row in range(rows):
        for copy in moved_queries[row]:
            arrive(copy)
        for index, result in enumerate(attend([qkv_in[0, peer, row] for peer in band_peers])):
            att_out[row, index] = result
        for copy in returned[row]:
            begin(copy)
        if row == final_row:
            for copy in direct[:-1]:
                begin(copy)
        if row >= 1:
            pass_on(row - 1)
        if row == final_row:
            settle(queries_end)
    load_output.wait()
    relay(0)
    pass_on(final_row)
    for row in range(1, rows):
        relay(row)
    for row in range(rows):
        finish(row)

    settle(len(opened))


def pair_shards(
    parts,
    bands,
    heads,
    latent,
    first_gain,
    first_shift,
    kernel,
    kernel_bias,
    second_gain,
    second_shift,
    projection,
    output_weight,
    output_bias,
):
    rows, width, local = latent.shape
    channels, tokens = local * heads, rows * width
    inner = projection.shape[2]
    vectors = [first_gain, first_shift, second_gain, second_shift, kernel_bias, output_bias]
    vmem = pl.BlockSpec(memory_space=pltpu.VMEM)
    hbm = pl.BlockSpec(memory_space=pl.ANY)
    result = jax.ShapeDtypeStruct((rows, local, width), jnp.bfloat16)
    copies = 160
    call = pl.pallas_call(
        functools.partial(pair_kernel, (parts, bands, heads, rows, local, width)),
        out_shape=(result, result),
        in_specs=[hbm] * 10,
        out_specs=(vmem, vmem),
        scratch_shapes=[
            pltpu.VMEM((3, 3, local, channels), jnp.bfloat16),
            pltpu.VMEM((3, channels, inner), jnp.bfloat16),
            pltpu.VMEM((3, inner, channels), jnp.bfloat16),
            pltpu.VMEM((local, inner * heads), jnp.bfloat16),
            pltpu.VMEM((heads, 6, 1, local), jnp.float32),
            pltpu.VMEM((6, channels, width), jnp.float32),
            pltpu.VMEM((bands * heads, 1, width), jnp.float32),
            pltpu.VMEM((bands * heads, 1, width), jnp.float32),
            pltpu.VMEM((rows + 2, channels, width), jnp.bfloat16),
            pltpu.VMEM((rows + 2, channels, width), jnp.bfloat16),
            pltpu.VMEM((3 * local, tokens), jnp.float32),
            pltpu.VMEM((rows, channels, width), jnp.bfloat16),
            pltpu.VMEM((channels, tokens), jnp.bfloat16),
            pltpu.VMEM((3, bands, rows, HEAD_SIZE, width), jnp.bfloat16),
            pltpu.VMEM((3, bands, rows, HEAD_SIZE, width), jnp.bfloat16),
            pltpu.VMEM((rows, bands - 1, HEAD_SIZE, width), jnp.bfloat16),
            pltpu.VMEM((rows, inner * heads, width), jnp.bfloat16),
        ]
        + [pltpu.VMEM((local,), jnp.float32)] * 6
        + [
            pltpu.SemaphoreType.DMA((10,)),
            pltpu.SemaphoreType.REGULAR((2,)),
            pltpu.SemaphoreType.DMA((copies,)),
            pltpu.SemaphoreType.DMA((copies,)),
        ],
        compiler_params=pltpu.CompilerParams(
            collective_id=0, has_side_effects=True, vmem_limit_bytes=60 << 20
        ),
    )
    wide, gained = call(
        jnp.transpose(latent, (0, 2, 1)),
        *vectors,
        jnp.transpose(kernel, (1, 2, 0, 3)),
        jnp.transpose(projection, (1, 0, 2)),
        output_weight,
    )
    top = jnp.finfo(jnp.bfloat16).max
    return tuple(jnp.minimum(jnp.transpose(made, (0, 2, 1)), top) for made in (wide, gained))


def solution(mesh):
    placed = (
        P(("groups", "band"), None, "head"),
        P("head"),
        P("head"),
        P("head", None, None, None),
        P("head"),
        P("head"),
        P("head"),
        P("band", None, "head"),
        P("head", None),
        P("head"),
    )
    parts, bands, heads = (mesh.shape[axis] for axis in ("groups", "band", "head"))
    paired = heads == 4 and bands > 1 and HEADS == heads * bands and CHANNELS % (16 * parts * heads) == 0
    body = functools.partial(pair_shards, parts, bands, heads) if paired else shards
    return jax.shard_map(
        body,
        mesh=mesh,
        in_specs=placed,
        out_specs=(P(("groups", "band"), None, "head"), P(("groups", "band"), None, "head")),
        check_vma=False,
    )
```

```python
import functools
import math

import jax
import jax.numpy as jnp
from jax import lax
from jax.experimental import pallas as pl
from jax.experimental.pallas import tpu as pltpu
from jax.sharding import PartitionSpec as P

CHANNELS = 1280
HEADS = 16
HEAD_SIZE = 64
NORM_GROUPS = 32


def padded_2(cells, sides, width):
    for axis, dim in sides:
        count = lax.axis_size(axis)
        ends = count - 1
        head = lax.slice_in_dim(cells, 0, width, axis=dim)
        tail = lax.slice_in_dim(cells, cells.shape[dim] - width, cells.shape[dim], axis=dim)
        cells = jnp.concatenate(
            [
                lax.ppermute(tail, axis, [(i, (i + 1) % count) for i in range(ends)]),
                cells,
                lax.ppermute(head, axis, [((i + 1) % count, i) for i in range(ends)]),
            ],
            axis=dim,
        )
    return cells


def normalize(values, gain, shift, group_width, count):
    band_rows, width, channels = values.shape
    grouped = values.reshape(band_rows * width, channels // group_width, group_width)
    mean = lax.psum(jnp.sum(grouped, axis=(0, 2)), "band") / count
    centered = grouped - mean[None, :, None]
    spread = lax.psum(jnp.sum(centered * centered, axis=(0, 2)), "band") / count
    scaled = centered * lax.rsqrt(spread + 1e-05)[None, :, None]
    return scaled.reshape(band_rows, width, channels) * gain + shift


def contract_last(left, right):
    return lax.dot_general(
        left, right, (((1,), (1,)), ((), ())), preferred_element_type=jnp.float32
    )


def kernel_block(padded, weights, band_rows, width):
    inputs = padded.shape[2]
    wide = jnp.pad(padded, ((0, 0), (1, 1), (0, 0)))
    summed = jnp.zeros((band_rows * width, weights.shape[0]), jnp.float32)
    for above in range(3):
        for beside in range(3):
            window = wide[above : above + band_rows, beside : beside + width, :].reshape(
                band_rows * width, inputs
            )
            summed = summed + contract_last(window, weights[:, above, beside, :])
    return summed


def shards(
    latent,
    first_gain,
    first_shift,
    kernel,
    kernel_bias,
    second_gain,
    second_shift,
    projection,
    output_weight,
    output_bias,
):
    band_rows, width, channels = latent.shape
    tokens = band_rows * width
    group_width = CHANNELS // NORM_GROUPS
    count = lax.axis_size("band") * band_rows * width * group_width
    outputs = kernel.shape[0]
    latent_wide = latent.astype(jnp.float32)
    activated = jax.nn.silu(
        normalize(latent_wide, first_gain, first_shift, group_width, count)
    ).astype(jnp.bfloat16)
    gathered = lax.all_gather(activated, "head", axis=2, tiled=True)
    padded = padded_2(gathered, (("band", 0),), 1)
    summed = kernel_block(padded, kernel, band_rows, width)
    convolved = (latent_wide + kernel_bias + summed.reshape(band_rows, width, outputs)).astype(
        jnp.bfloat16
    )
    normed = normalize(
        convolved.astype(jnp.float32), second_gain, second_shift, group_width, count
    ).astype(jnp.bfloat16)
    features = lax.all_gather(normed, "head", axis=2, tiled=True).reshape(tokens, CHANNELS)
    local_inner = projection.shape[2]
    local_heads = local_inner // HEAD_SIZE
    piece = lax.all_gather(projection, "band", axis=0, tiled=True)
    projected = jnp.dot(
        features, piece.reshape(piece.shape[0], 3 * local_inner), preferred_element_type=jnp.float32
    )
    projected = projected.astype(jnp.bfloat16).reshape(tokens, 3, local_inner)
    query = projected[:, 0].reshape(tokens, local_heads, HEAD_SIZE)
    key_value = projected[:, 1:]
    factor = HEAD_SIZE ** (-0.5)
    piece = lax.all_gather(key_value, "band", axis=0, tiled=True)
    running = jnp.full((local_heads, tokens), -1e30, jnp.float32)
    keys = piece[:, 0].reshape(piece.shape[0], local_heads, HEAD_SIZE)
    values = piece[:, 1].reshape(piece.shape[0], local_heads, HEAD_SIZE)
    scores = jnp.einsum("qhd,khd->hqk", query, keys, preferred_element_type=jnp.float32) * factor
    highest = jnp.maximum(running, jnp.max(scores, axis=2))
    weights = jnp.exp(scores - highest[:, :, None])
    total = jnp.sum(weights, axis=2)
    summed_values = jnp.einsum(
        "hqk,khd->hqd", weights.astype(jnp.bfloat16), values, preferred_element_type=jnp.float32
    )
    running, total, summed_values = (highest, total, summed_values)
    attention = (
        jnp.transpose(summed_values / total[:, :, None], (1, 0, 2))
        .reshape(tokens, local_inner)
        .astype(jnp.bfloat16)
    )
    outgoing = contract_last(lax.all_gather(attention, "head", axis=1, tiled=True), output_weight)
    attended = (
        convolved.astype(jnp.float32) + output_bias + outgoing.reshape(band_rows, width, outputs)
    )
    return (convolved, attended.astype(jnp.bfloat16))


def pair_kernel(
    shape,
    lat_hbm,
    gain_a,
    shift_a,
    gain_b,
    shift_b,
    bias_a,
    bias_b,
    kw_hbm,
    pj_hbm,
    ow_hbm,
    wide_ref,
    gain_ref,
    kw,
    pw,
    turned,
    ow,
    par,
    spread_par,
    stat_a,
    stat_b,
    raw_in,
    grid_in,
    sums,
    conv_in,
    feats,
    qkv_out,
    qkv_in,
    att_out,
    att_in,
    vector_0,
    vector_1,
    vector_2,
    vector_3,
    vector_4,
    vector_5,
    local_sem,
    entry_sem,
    send_sem,
    recv_sem,
):
    parts, bands, heads, rows, local, width = shape
    channels = local * heads
    tokens = rows * width
    group_width = CHANNELS // NORM_GROUPS
    groups_here = local // group_width
    pair = 2 * local
    g, b, h = lax.axis_index("groups"), lax.axis_index("band"), lax.axis_index("head")
    sibling = h + 1 - 2 * lax.rem(h, 2)
    cross = lax.rem(h + 2, heads)
    far = lax.rem(sibling + 2, heads)
    has_above, has_below = b > 0, b < bands - 1
    above, below = lax.rem(b + bands - 1, bands), lax.rem(b + 1, bands)
    mesh_id = pl.DeviceIdType.MESH
    used = [0]

    def remote(src, dst, groups=None, band=None, head=None):
        index = used[0]
        used[0] += 1
        return pltpu.make_async_remote_copy(
            src_ref=src,
            dst_ref=dst,
            send_sem=send_sem.at[index],
            recv_sem=recv_sem.at[index],
            device_id=(
                g if groups is None else groups,
                b if band is None else band,
                h if head is None else head,
            ),
            device_id_type=mesh_id,
        )

    opened = []

    def begin(copy, sends=None):
        opened.append((copy, sends))
        if sends is None:
            copy.start()
        else:

            @pl.when(sends)
            def _():
                copy.start()

    settled = [0]

    def settle(until):
        for copy, sends in opened[settled[0] : until]:
            if sends is None:
                copy.wait_send()
            else:

                @pl.when(sends)
                def _(copy=copy):
                    copy.wait_send()

        settled[0] = max(settled[0], until)

    def arrive(copy, receives=None):
        if receives is None:
            copy.wait_recv()
        else:

            @pl.when(receives)
            def _():
                copy.wait_recv()

    def channel_rows(shard):
        return pl.ds(pl.multiple_of(shard * local, local), local)

    band_peers = [lax.rem(b + 2, bands), bands - 1 - b, b + 1 - 2 * lax.rem(b, 2)]
    part_peers = [lax.rem(g + step, parts) for step in range(1, parts)]
    mine, crossed, sibs, fars = (channel_rows(s) for s in (h, cross, sibling, far))

    barrier = pltpu.get_barrier_semaphore()
    close = [(g, b, sibling), (g, b, cross), (g, b, far)] + [(peer, b, h) for peer in part_peers]
    for neighbour in close:
        pl.semaphore_signal(barrier, inc=1, device_id=neighbour, device_id_type=mesh_id)

    def tell(sem):
        @pl.when(has_above)
        def _():
            pl.semaphore_signal(sem, inc=1, device_id=(g, above, h), device_id_type=mesh_id)

        @pl.when(has_below)
        def _():
            pl.semaphore_signal(sem, inc=1, device_id=(g, below, h), device_id_type=mesh_id)

    def told(sem, others=0):
        inside = jnp.logical_and(has_above, has_below)

        @pl.when(inside)
        def _():
            pl.semaphore_wait(sem, others + 2)

        @pl.when(jnp.logical_not(inside))
        def _():
            pl.semaphore_wait(sem, others + 1)

    tell(barrier)

    load_lat = pltpu.make_async_copy(lat_hbm, raw_in.at[pl.ds(1, rows), mine, :], local_sem.at[0])
    load_lat.start()
    held_vectors = (vector_0, vector_1, vector_2, vector_3, vector_4, vector_5)
    vectors = (gain_a, shift_a, gain_b, shift_b, bias_a, bias_b)
    load_vectors = [
        pltpu.make_async_copy(vector, held, local_sem.at[4 + index])
        for index, (vector, held) in enumerate(zip(vectors, held_vectors))
    ]
    for load in load_vectors:
        load.start()
    load_kernel = pltpu.make_async_copy(kw_hbm, kw, local_sem.at[1])
    load_rows = pltpu.make_async_copy(pj_hbm, pw.at[:, channel_rows(b), :], local_sem.at[2])
    load_output = pltpu.make_async_copy(ow_hbm, ow, local_sem.at[3])
    load_kernel.start()
    load_rows.start()
    load_output.start()

    count = rows * width * group_width
    both = 2 * groups_here
    sub16 = lax.broadcasted_iota(jnp.int32, (both, width), 0)
    lane16 = lax.broadcasted_iota(jnp.int32, (both, width), 1)
    sub8 = lax.broadcasted_iota(jnp.int32, (groups_here, width), 0)
    lane8 = lax.broadcasted_iota(jnp.int32, (groups_here, width), 1)

    def statistics(buffer, first):
        values = [
            buffer[first + row, mine, :].astype(jnp.float32).reshape(groups_here, group_width, width)
            for row in range(rows)
        ]
        total = sum(jnp.sum(value, axis=1) for value in values)
        mean = jnp.sum(total, axis=1, keepdims=True) / count
        mean = jnp.broadcast_to(mean, (groups_here, width))
        squares = 0.0
        for value in values:
            centered = value - mean[:, None, :]
            squares = squares + jnp.sum(centered * centered, axis=1)
        squares = jnp.broadcast_to(jnp.sum(squares, axis=1, keepdims=True), (groups_here, width))
        stacked = jnp.concatenate([mean, squares], axis=0)
        return jnp.sum(jnp.where(sub16 == lane16, stacked, 0.0), axis=0, keepdims=True)

    def combined(stat):
        found = []
        for shard in (h, sibling, cross, far):
            pieces = [stat[band * heads + shard] for band in range(bands)]
            total = sum(pieces)
            mean = total / bands
            offsets = sum((piece - mean) * (piece - mean) for piece in pieces)
            spread = pltpu.roll(jnp.broadcast_to(total, (8, width)), width - groups_here, 1)[:1]
            scale = lax.rsqrt((spread + offsets * count) / (count * bands) + 1e-05)
            pair_of = []
            for line in (mean, scale):
                wide = jnp.broadcast_to(line, (groups_here, width))
                column = jnp.sum(jnp.where(sub8 == lane8, wide, 0.0), axis=1, keepdims=True)
                pair_of.append(jnp.broadcast_to(column, (groups_here, width)))
            found.append(pair_of)
        return found

    def normalized(value, stats, which, span):
        mean, scale = stats
        grouped = value.astype(jnp.float32).reshape(groups_here, group_width, width)
        scaled = (grouped - mean[:, None, :]) * scale[:, None, :]
        return scaled.reshape(local, width) * spread_par[2 * which, span, :] + spread_par[
            2 * which + 1, span, :
        ]

    load_lat.wait()
    stat_a[b * heads + h] = statistics(raw_in, 1)
    for index, load in enumerate(load_vectors):
        load.wait()
        par[h, index] = held_vectors[index][...].reshape(1, local)

    told(barrier, len(close))

    def gather_pieces(buffer, pieces):
        sent = []
        for piece in pieces:
            own = buffer.at[piece, mine, :]
            there = buffer.at[piece, crossed, :]
            sent.append(
                (
                    remote(own, own, head=cross),
                    remote(own, own, head=sibling),
                    remote(there, there, head=sibling),
                )
            )
        return sent

    share = local // parts

    def share_rows(band, part):
        return pl.ds(pl.multiple_of(band * local + part * share, share), share)

    hops = []
    passed = []
    for kind in range(3):
        steps = []
        for hop in range(1, bands):
            two = []
            for sign, peer in ((1, below), (-1, above)):
                held = lax.rem(b - sign * (hop - 1) + bands, bands)
                got = lax.rem(b - sign * hop + bands, bands)
                if sign > 0:
                    sends = jnp.logical_and(b < bands - 1, b >= hop - 1)
                    receives = b >= hop
                else:
                    sends = jnp.logical_and(b > 0, b + hop - 1 < bands)
                    receives = b + hop < bands
                if hop == 1:
                    source = pj_hbm.at[kind, pl.ds(pl.multiple_of(g * share, share), share), :]
                else:
                    source = pw.at[kind, share_rows(held, g), :]
                move = remote(source, pw.at[kind, share_rows(held, g), :], band=peer)
                two.append((move, sends, receives, got))
            steps.append(two)
        hops.append(steps)
        passed.append([])

    def send_hop(kind, index):
        for move, sends, _, _ in hops[kind][index]:
            begin(move, sends)

    def take_hop(kind, index):
        for move, _, receives, _ in hops[kind][index]:
            arrive(move, receives)
        if index + 1 < len(hops[kind]):
            send_hop(kind, index + 1)
        for _, _, receives, got in hops[kind][index]:
            onward = pw.at[kind, share_rows(got, g), :]
            for peer in part_peers:
                move = remote(onward, onward, groups=peer)
                begin(move, receives)
                passed[kind].append((move, receives))

    plan = {'pre': '+K0', 'bs': '+V0', 'G': '-K0 +Q0', 'H1': '-V0 -K1', 'mid': '-Q0', 'T': '-K2 -V1', 'T2': '-Q1', 'R0': '-V2', 'R1': '-Q2'}

    def go(point):
        for word in plan.get(point, "").split():
            kind, index = "QKV".index(word[1]), int(word[2])
            if word[0] == "+":
                send_hop(kind, index)
            else:
                take_hop(kind, index)

    own_row = stat_a.at[b * heads + h]
    near_stats = [remote(own_row, own_row, head=peer) for peer in (cross, far, sibling)]
    near_par = [
        remote(par.at[h, pl.ds(0, 4)], par.at[h, pl.ds(0, 4)], head=peer)
        for peer in (cross, far, sibling)
    ]
    edges = (pl.ds(rows, 1), pl.ds(1, 1), pl.ds(2, rows - 2))
    gathered = gather_pieces(raw_in, edges)
    halo = []
    for source, target, peer, sends, receives in (
        (rows, 0, below, has_below, has_above),
        (1, rows + 1, above, has_above, has_below),
    ):
        for shard in (mine, crossed):
            move = remote(raw_in.at[source, shard, :], raw_in.at[target, shard, :], band=peer)
            onward = raw_in.at[target, shard, :]
            halo.append((move, remote(onward, onward, head=sibling), sends, receives))
    for copy in near_stats:
        begin(copy)
    for copy in near_par:
        begin(copy)
    tell(entry_sem.at[0])
    for to_cross, to_sibling, _ in gathered:
        begin(to_cross)
        begin(to_sibling)
    for index in (0, 2):
        move, _, sends, _ = halo[index]
        begin(move, sends)

    go('pre')
    told(entry_sem.at[0])
    tell(entry_sem.at[1])
    for copy in near_stats:
        arrive(copy)
    told(entry_sem.at[1])
    block = stat_a.at[pl.ds(b * heads, heads)]
    band_stats = [remote(block, block, band=peer) for peer in band_peers]
    for copy in band_stats:
        begin(copy)
    go('bs')

    for copy in near_par:
        arrive(copy)
    blocks = -(-local // width)
    lines = []
    for shard in range(heads):
        for index in range(4):
            lines.append(par[shard, index])
    lines += [par[h, 4], par[h, 5]]
    gap = jnp.zeros((1, blocks * width - local), jnp.float32)
    flat = []
    for line in lines:
        line = jnp.concatenate([line, gap], axis=1)
        flat += [line[:, k * width : (k + 1) * width] for k in range(blocks)]
    flat.append(jnp.zeros((-len(flat) % width, width), jnp.float32))
    columns = jnp.concatenate(flat, axis=0).T

    def column(index):
        pieces = [columns[:, index * blocks + k : index * blocks + k + 1] for k in range(blocks)]
        return jnp.broadcast_to(jnp.concatenate(pieces, axis=0)[:local], (local, width))

    for index in range(2):
        for shard in range(heads):
            spread_par[index, shard * local : (shard + 1) * local, :] = column(shard * 4 + index)
    for index in range(2):
        to_cross, _, onward = gathered[index]
        arrive(to_cross)
        begin(onward)
        move, _, sends, _ = halo[2 * index + 1]
        begin(move, sends)
    for index in (0, 2):
        move, onward, _, receives = halo[index]
        arrive(move, receives)
        begin(onward, receives)
    for target, receives in ((0, has_above), (rows + 1, has_below)):

        @pl.when(jnp.logical_not(receives))
        def _(target=target):
            grid_in[target] = jnp.zeros((channels, width), jnp.bfloat16)

    go('G')
    for index in range(2, 4):
        for shard in range(heads):
            spread_par[index, shard * local : (shard + 1) * local, :] = column(shard * 4 + index)
    for index in range(2):
        spread_par[4 + index, :local, :] = column(heads * 4 + index)

    to_cross, _, onward = gathered[2]
    arrive(to_cross)
    begin(onward)
    for copy in band_stats:
        arrive(copy)
    first = combined(stat_a)

    def activate(row, slot, span):
        value = 0.5 * normalized(raw_in[row, span, :], first[slot], 0, span)
        grid_in[row, span, :] = (value + value * jnp.tanh(value)).astype(jnp.bfloat16)

    def activate_edge(target, receives, slots):
        @pl.when(receives)
        def _():
            for slot, span in slots:
                activate(target, slot, span)

    def half(which):
        return pl.ds(pl.multiple_of(which * pair, pair), pair)

    def convolve(which, overs, fresh, chosen=range(rows)):
        span = half(which)
        place = slice(chosen[0] * width, (chosen[-1] + 1) * width)
        total = None
        for over in overs:
            window = jnp.concatenate([grid_in[over + row, span, :] for row in chosen], axis=1)
            weights = kw[over, :, :, span].reshape(3 * local, pair)
            part = jnp.dot(weights, window, preferred_element_type=jnp.float32)
            total = part if total is None else total + part
        if not fresh:
            total = sums[:, place] + total
        sums[:, place] = total

    this_half, other_half = h // 2, cross // 2
    near_slots = ((0, mine), (1, sibs))
    far_slots = ((2, crossed), (3, fars))
    for _, to_sibling, _ in gathered:
        arrive(to_sibling)
    for row in range(rows):
        for slot, span in near_slots:
            activate(1 + row, slot, span)
    go('C')
    load_kernel.wait()
    convolve(this_half, (1,), True)
    for index in (0, 2):
        _, onward, _, receives = halo[index]
        arrive(onward, receives)
    activate_edge(0, has_above, near_slots)
    activate_edge(rows + 1, has_below, near_slots)
    convolve(this_half, (0, 2), False)
    for index in (1, 3):
        move, onward, _, receives = halo[index]
        arrive(move, receives)
        begin(onward, receives)
    for _, _, onward in gathered:
        arrive(onward)
    for row in range(rows):
        for slot, span in far_slots:
            activate(1 + row, slot, span)
    go('H1')
    early = len(opened)
    convolve(other_half, (1,), False)
    for index in (1, 3):
        _, onward, _, receives = halo[index]
        arrive(onward, receives)
    activate_edge(0, has_above, far_slots)
    activate_edge(rows + 1, has_below, far_slots)
    go('mid')
    place = lax.broadcasted_iota(jnp.int32, (local, width), 1)
    normed = gather_pieces(conv_in, tuple(pl.ds(row, 1) for row in range(rows)))

    def close_row(row):
        span = slice(row * width, (row + 1) * width)
        left = jnp.where(place == 0, 0.0, pltpu.roll(sums[:local, span], 1, 1))
        right = jnp.where(place == width - 1, 0.0, pltpu.roll(sums[2 * local :, span], width - 1, 1))
        value = (
            raw_in[1 + row, mine, :].astype(jnp.float32)
            + spread_par[4, :local, :]
            + (sums[local : 2 * local, span] + left + right)
        )
        conv_in[row, mine, :] = value.astype(jnp.bfloat16)
        wide_ref[row] = value.astype(jnp.bfloat16)

    def send_row(row):
        begin(normed[row][0])
        begin(normed[row][1])

    convolve(other_half, (0, 2), False, range(1))
    close_row(0)
    send_row(0)
    convolve(other_half, (0, 2), False, range(1, rows))
    for row in range(1, rows):
        close_row(row)
    stat_b[b * heads + h] = statistics(conv_in, 0)
    own_row = stat_b.at[b * heads + h]
    all_stats = [
        remote(own_row, own_row, band=lax.rem(b + up, bands), head=lax.rem(h + over, heads))
        for up in range(bands - 1, -1, -1)
        for over in range(heads - 1, -1, -1)
        if up or over
    ]
    for copy in all_stats:
        begin(copy)
    for row in range(1, rows):
        send_row(row)
    load_rows.wait()
    go('T')
    arrive(normed[0][0])
    begin(normed[0][2])
    go('T2')
    settle(early)
    for copy in all_stats:
        arrive(copy)
    second = combined(stat_b)
    arrive(normed[1][0])
    begin(normed[1][2])
    go('T3')
    for move, receives in passed[1]:
        arrive(move, receives)

    def normalize_row(row):
        arrive(normed[row][1])
        span = slice(row * width, (row + 1) * width)
        for slot, shard in ((0, mine), (1, sibs), (2, crossed)):
            feats[shard, span] = normalized(conv_in[row, shard, :], second[slot], 1, shard).astype(
                jnp.bfloat16
            )
        arrive(normed[row][2])
        feats[fars, span] = normalized(conv_in[row, fars, :], second[3], 1, fars).astype(jnp.bfloat16)

    def project(kind, span):
        return jnp.dot(turned[kind], feats[:, span], preferred_element_type=jnp.float32).astype(
            jnp.bfloat16
        )

    def place_heads(kind, made, chosen):
        for head in range(bands):
            for index, row in enumerate(chosen):
                qkv_out[kind, head, row] = made[
                    head * HEAD_SIZE : (head + 1) * HEAD_SIZE, index * width : (index + 1) * width
                ]

    def spread_rows(kind, row, size):
        chosen = pl.ds(row, size)
        qkv_in[kind, b, chosen] = qkv_out[kind, b, chosen]
        moves = [
            remote(qkv_out.at[kind, peer, chosen], qkv_in.at[kind, b, chosen], band=peer)
            for peer in band_peers
        ]
        for copy in moves:
            begin(copy)
        return moves

    turned[1] = pw[1].T
    moved_keys = []
    early = len(opened)
    for row in range(rows):
        normalize_row(row)
        if row + 2 < rows:
            arrive(normed[row + 2][0])
            begin(normed[row + 2][2])
        place_heads(1, project(1, slice(row * width, (row + 1) * width)), (row,))
        moved_keys += spread_rows(1, row, 1)
        go('R%d' % row)
    go('RE')
    everything = slice(0, tokens)
    for move, receives in passed[2]:
        arrive(move, receives)
    turned[2] = pw[2].T
    place_heads(2, project(2, everything), range(rows))
    moved_values = spread_rows(2, 0, rows)
    for move, receives in passed[0]:
        arrive(move, receives)
    turned[0] = pw[0].T
    place_heads(0, project(0, everything), range(rows))
    moved_queries = [spread_rows(0, row, 1) for row in range(rows)]

    inner = bands * HEAD_SIZE
    factor = HEAD_SIZE ** (-0.5) * math.log2(math.e)

    def feature_rows(shard):
        return pl.ds(pl.multiple_of(shard * inner, inner), inner)

    own_features = pl.ds(pl.multiple_of(h * inner + b * HEAD_SIZE, HEAD_SIZE), HEAD_SIZE)
    final_row = rows - 1
    returned = [
        [
            remote(att_out.at[row, index], att_in.at[row, own_features, :], band=peer)
            for index, peer in enumerate(band_peers)
        ]
        for row in range(rows)
    ]
    direct = [
        remote(
            att_out.at[final_row, index],
            att_in.at[final_row, own_features, :],
            band=peer,
            head=cross,
        )
        for index, peer in enumerate(band_peers)
    ]
    own_final = att_in.at[final_row, own_features, :]
    direct.append(remote(own_final, own_final, head=cross))
    final = []
    for row in range(rows):
        own = att_in.at[row, feature_rows(h), :]
        there = att_in.at[row, feature_rows(cross), :]
        to_cross = remote(own, own, head=cross) if row < final_row else None
        final.append(
            (to_cross, remote(own, own, head=sibling), remote(there, there, head=sibling))
        )

    def pass_on(row):
        for copy in returned[row]:
            arrive(copy)
        if row < final_row:
            begin(final[row][0])
        begin(final[row][1])

    def relay(row):
        for copy in direct if row == final_row else final[row][:1]:
            arrive(copy)
        begin(final[row][2])

    def finish(row):
        arrive(final[row][1])
        arrive(final[row][2])
        outgoing = jnp.dot(ow[...], att_in[row], preferred_element_type=jnp.float32)
        gain_ref[row] = (
            conv_in[row, mine, :].astype(jnp.float32) + spread_par[5, :local, :] + outgoing
        ).astype(jnp.bfloat16)

    settle(early)
    for copy in moved_keys:
        arrive(copy)
    keys = jnp.concatenate(
        [qkv_in[1, source, row] for source in range(bands) for row in range(rows)], axis=1
    ).T
    for copy in moved_values:
        arrive(copy)
    values = jnp.concatenate(
        [qkv_in[2, source, row] for source in range(bands) for row in range(rows)], axis=1
    )

    def attend(pieces):
        query = jnp.concatenate(pieces, axis=1)
        scores = jnp.dot(keys, query, preferred_element_type=jnp.float32)
        top = jnp.max(scores, axis=0, keepdims=True)
        heavy = jnp.exp2((scores - top) * factor)
        total = jnp.sum(heavy, axis=0, keepdims=True)
        mixed = jnp.dot(values, heavy.astype(jnp.bfloat16), preferred_element_type=jnp.float32)
        result = (mixed / total).astype(jnp.bfloat16)
        return [result[:, k * width : (k + 1) * width] for k in range(len(pieces))]

    for row, result in enumerate(attend([qkv_out[0, b, row] for row in range(rows)])):
        att_in[row, own_features, :] = result
    settle(len(opened) - rows * len(band_peers))
    queries_end = len(opened)
    begin(direct[-1])
    for row in range(rows):
        for copy in moved_queries[row]:
            arrive(copy)
        for index, result in enumerate(attend([qkv_in[0, peer, row] for peer in band_peers])):
            att_out[row, index] = result
        for copy in returned[row]:
            begin(copy)
        if row == final_row:
            for copy in direct[:-1]:
                begin(copy)
        if row >= 1:
            pass_on(row - 1)
        if row == final_row:
            settle(queries_end)
    load_output.wait()
    relay(0)
    pass_on(final_row)
    for row in range(1, rows):
        relay(row)
    for row in range(rows):
        finish(row)

    settle(len(opened))


def pair_shards(
    parts,
    bands,
    heads,
    latent,
    first_gain,
    first_shift,
    kernel,
    kernel_bias,
    second_gain,
    second_shift,
    projection,
    output_weight,
    output_bias,
):
    rows, width, local = latent.shape
    channels, tokens = local * heads, rows * width
    inner = projection.shape[2]
    vectors = [first_gain, first_shift, second_gain, second_shift, kernel_bias, output_bias]
    vmem = pl.BlockSpec(memory_space=pltpu.VMEM)
    hbm = pl.BlockSpec(memory_space=pl.ANY)
    result = jax.ShapeDtypeStruct((rows, local, width), jnp.bfloat16)
    copies = 160
    call = pl.pallas_call(
        functools.partial(pair_kernel, (parts, bands, heads, rows, local, width)),
        out_shape=(result, result),
        in_specs=[hbm] * 10,
        out_specs=(vmem, vmem),
        scratch_shapes=[
            pltpu.VMEM((3, 3, local, channels), jnp.bfloat16),
            pltpu.VMEM((3, channels, inner), jnp.bfloat16),
            pltpu.VMEM((3, inner, channels), jnp.bfloat16),
            pltpu.VMEM((local, inner * heads), jnp.bfloat16),
            pltpu.VMEM((heads, 6, 1, local), jnp.float32),
            pltpu.VMEM((6, channels, width), jnp.float32),
            pltpu.VMEM((bands * heads, 1, width), jnp.float32),
            pltpu.VMEM((bands * heads, 1, width), jnp.float32),
            pltpu.VMEM((rows + 2, channels, width), jnp.bfloat16),
            pltpu.VMEM((rows + 2, channels, width), jnp.bfloat16),
            pltpu.VMEM((3 * local, tokens), jnp.float32),
            pltpu.VMEM((rows, channels, width), jnp.bfloat16),
            pltpu.VMEM((channels, tokens), jnp.bfloat16),
            pltpu.VMEM((3, bands, rows, HEAD_SIZE, width), jnp.bfloat16),
            pltpu.VMEM((3, bands, rows, HEAD_SIZE, width), jnp.bfloat16),
            pltpu.VMEM((rows, bands - 1, HEAD_SIZE, width), jnp.bfloat16),
            pltpu.VMEM((rows, inner * heads, width), jnp.bfloat16),
        ]
        + [pltpu.VMEM((local,), jnp.float32)] * 6
        + [
            pltpu.SemaphoreType.DMA((10,)),
            pltpu.SemaphoreType.REGULAR((2,)),
            pltpu.SemaphoreType.DMA((copies,)),
            pltpu.SemaphoreType.DMA((copies,)),
        ],
        compiler_params=pltpu.CompilerParams(
            collective_id=0, has_side_effects=True, vmem_limit_bytes=60 << 20
        ),
    )
    wide, gained = call(
        jnp.transpose(latent, (0, 2, 1)),
        *vectors,
        jnp.transpose(kernel, (1, 2, 0, 3)),
        jnp.transpose(projection, (1, 0, 2)),
        output_weight,
    )
    top = jnp.finfo(jnp.bfloat16).max
    return tuple(jnp.minimum(jnp.transpose(made, (0, 2, 1)), top) for made in (wide, gained))


def solution(mesh):
    placed = (
        P(("groups", "band"), None, "head"),
        P("head"),
        P("head"),
        P("head", None, None, None),
        P("head"),
        P("head"),
        P("head"),
        P("band", None, "head"),
        P("head", None),
        P("head"),
    )
    parts, bands, heads = (mesh.shape[axis] for axis in ("groups", "band", "head"))
    paired = heads == 4 and bands > 1 and HEADS == heads * bands and CHANNELS % (16 * parts * heads) == 0
    body = functools.partial(pair_shards, parts, bands, heads) if paired else shards
    return jax.shard_map(
        body,
        mesh=mesh,
        in_specs=placed,
        out_specs=(P(("groups", "band"), None, "head"), P(("groups", "band"), None, "head")),
        check_vma=False,
    )
```
